512 devices in a mesh: gx: 16 (over x, z_hi), gy: 32 (over y, z_lo, core).
Axes of the slice: x: 4, y: 8, z: 8 (z_hi: 4, z_lo: 2; z = z_hi * 2 + z_lo), core: 2. Of those that a mesh axis runs over, the one named last changes fastest.
Arguments:
- prev_block: float32 [3, 8, 128, 256, 128], P(None, None, 'gx', 'gy'), may hold values from -20 to 20
- block: float32 [3, 8, 128, 256, 128], P(None, None, 'gx', 'gy'), may hold values from -20 to 20
- hop_seed: int32 [3, 128, 256, 128], P(None, 'gx', 'gy'), may hold values from 0 to 15
- levels: int32 [128, 256, 128], P('gx', 'gy'), may hold values from 0 to 15
- hop_table: float32 [3, 16, 3, 3], replicated, may hold values from -3 to 3
- onsite_table: float32 [16, 3], replicated, may hold values from -2 to 2
Outputs:
- next_block: float32 [3, 8, 128, 256, 128], P(None, None, 'gx', 'gy')
- alpha: float32 [8, 8], replicated
- beta: float32 [8, 8], replicated
The draws below stay inside these ranges and needn't reach their ends.
All inputs are finite; a program needn't handle non-finite values.
Results may differ from the reference program's by a relative error of at most 0.0003.
Values sent between devices are 32-bit elements; how exact they have to be, the bound alone decides.
A program may use at most 64 MiB of HBM per device.

```python
import jax
import jax.numpy as jnp
from jax import lax

NZ = 128
ORB = 3
BLOCK = 8
KINDS = 16
LEVELS = 16
NX = 128
NY = 256


def pair_fields(key):
    shape = (ORB, BLOCK, NX, NY, NZ)
    key_one = jax.random.fold_in(key, 101)
    key_two = jax.random.fold_in(key, 102)
    first = jnp.clip(jax.random.normal(key_one, shape, jnp.float32), -5.0, 5.0)
    second = jnp.clip(jax.random.normal(key_two, shape, jnp.float32), -5.0, 5.0)
    xpos = jnp.arange(NX, dtype=jnp.float32)[:, None, None] / NX
    ypos = jnp.arange(NY, dtype=jnp.float32)[None, :, None] / NY
    ramp = 0.6 * jnp.exp(jnp.log(3.0) * 0.5 * (xpos + ypos))
    return (ramp * first, ramp * (0.4 * first + second))


def draw_prev_block(key, part):
    return pair_fields(key)[0]


def draw_block(key, part):
    return pair_fields(key)[1]


def touch_ends(array, stream_key, least, top_value):
    longest = array.shape.index(max(array.shape))
    spots = []
    for shift in (0, 1):
        where = [jax.random.randint(jax.random.fold_in(stream_key, axis), (), 0, length) for axis, length in enumerate(array.shape)]
        where[longest] = (where[longest] + shift) % array.shape[longest]
        spots.append(tuple(where))
    return array.at[spots[0]].set(least).at[spots[1]].set(top_value)


def normal_values(rng, shape, scale, bound, held_as=jnp.bfloat16):
    return jnp.clip(scale * jax.random.normal(rng, shape, jnp.float32), -bound, bound).astype(held_as)


def setup_inputs(seed: int = 0) -> dict:
    splits = jax.random.split(jax.random.key(seed), 7)
    return {
        "prev_block": draw_prev_block(jax.random.fold_in(splits[6], 71), 0),
        "block": draw_block(jax.random.fold_in(splits[6], 71), 0),
        "hop_seed": touch_ends(jax.random.randint(splits[2], (3, NX, NY, NZ), 0, KINDS), jax.random.fold_in(splits[2], 1), 0, KINDS - 1).astype(jnp.int32),
        "levels": touch_ends(jax.random.randint(splits[3], (NX, NY, NZ), 0, LEVELS), jax.random.fold_in(splits[3], 1), 0, LEVELS - 1).astype(jnp.int32),
        "hop_table": normal_values(splits[4], (3, KINDS, ORB, ORB), 0.5, 3.0, jnp.float32),
        "onsite_table": jnp.clip(jax.random.uniform(splits[5], (LEVELS, ORB), jnp.float32, -2.0, 2.0), -2.0, 2.0),
    }


HIGH = lax.Precision.HIGHEST

def apply_ham(field, hop_seed, levels, hop_table, onsite_table):
    energy = jnp.moveaxis(onsite_table[levels], -1, 0)
    image = energy[:, None] * field
    for direction in range(3):
        bonds = jnp.moveaxis(hop_table[direction][hop_seed[direction]], (-2, -1), (0, 1))
        ahead = jnp.roll(field, -1, axis=2 + direction)
        image = image + jnp.einsum('abxyz,bnxyz->anxyz', bonds, ahead, precision=HIGH)
        carried = jnp.einsum('abxyz,anxyz->bnxyz', bonds, field, precision=HIGH)
        image = image + jnp.roll(carried, 1, axis=2 + direction)
    return image

def inner(left, right):
    count = left.shape[0] * left.shape[2] * left.shape[3] * left.shape[4]
    return jnp.einsum('omxyz,onxyz->mn', left, right, precision=HIGH) / count

def combine(basis, coeffs):
    return jnp.einsum('okxyz,kn->onxyz', basis, coeffs, precision=HIGH)

def reference(prev_block, block, hop_seed, levels, hop_table, onsite_table):
    product = apply_ham(block, hop_seed, levels, hop_table, onsite_table)
    basis = jnp.concatenate([prev_block, block], axis=1)
    first = inner(basis, product)
    alpha = first[BLOCK:]
    residual_one = product - combine(basis, first)
    second = inner(basis, residual_one)
    residual_two = residual_one - combine(basis, second)
    gram = inner(residual_two, residual_two)
    lower = jnp.linalg.cholesky(gram)
    lower_inv = jax.scipy.linalg.solve_triangular(lower, jnp.eye(BLOCK, dtype=jnp.float32), lower=True)
    next_block = jnp.einsum('omxyz,nm->onxyz', residual_two, lower_inv, precision=HIGH)
    return (next_block, alpha, lower.T)
```

```python
import functools

import jax
import jax.numpy as jnp
from jax import lax
from jax.experimental import pallas as pl
from jax.experimental.pallas import tpu as pltpu
from jax.sharding import PartitionSpec as P

HIGH = lax.Precision.HIGHEST
MESH = pl.DeviceIdType.MESH
ORB, WIDTH, SIDE, LANES, KINDS = 3, 8, 8, 128, 16
ROWS = SIDE * SIDE
FIELDS = 3 * WIDTH

DIGITS = {"x": 4, "zh": 4, "y": 8, "zl": 2, "core": 2}
STAGES = (("core", "y"), ("x", "zh", "zl"))


def position():
    gx, gy = lax.axis_index("gx"), lax.axis_index("gy")
    return {"x": gx // 4, "zh": gx % 4, "y": gy // 4, "zl": (gy // 2) % 2, "core": gy % 2}


def device(pos):
    return (pos["x"] * 4 + pos["zh"], pos["y"] * 4 + pos["zl"] * 2 + pos["core"])


def group_size(dims):
    size = 1
    for dim in dims:
        size *= DIGITS[dim]
    return size


def member(pos, dims):
    index = 0
    for dim in dims:
        index = index * DIGITS[dim] + pos[dim]
    return index


def offsets(dims):
    found = []
    for k in range(1, group_size(dims)):
        off, rest = {}, k
        for dim in reversed(dims):
            off[dim] = rest % DIGITS[dim]
            rest //= DIGITS[dim]
        hops = 0
        if "y" in off:
            hops += min(off["y"], 8 - off["y"])
        if "x" in off:
            hops += min(off["x"], 4 - off["x"])
        if "zh" in off:
            z = (off["zh"] * 2 + off.get("zl", 0)) % 8
            hops += min(z, 8 - z)
        found.append((-hops, k, off))
    return [off for _, _, off in sorted(found, key=lambda t: t[:2])]


def peer(pos, off):
    return {d: (pos[d] + off[d]) % DIGITS[d] if off.get(d) else pos[d] for d in pos}


def iota(axis):
    return lax.broadcasted_iota(jnp.int32, (8, LANES), axis)


def fold_rows(parts):
    row = iota(0)
    for bit in (1, 2, 4):
        low = (row & bit) == 0
        parts = [
            jnp.where(low, a, b) + pltpu.roll(jnp.where(low, b, a), bit, axis=0)
            for a, b in zip(parts[0::2], parts[1::2])
        ]
    return parts[0]


def inner_rows(fields, first, others, lane, sums):
    def step(x, acc):
        rows = pl.ds(pl.multiple_of(8 * x + 8, 8), 8)
        for orb in range(ORB):
            left = [fields[orb, first + r, rows, :] for r in range(4)]
            right = [fields[orb, others + s, rows, :] for s in range(8)]
            acc = [acc[r * 8 + s] + left[r] * right[s] for r in range(4) for s in range(8)]
        return tuple(acc)

    zero = jnp.zeros((8, LANES), jnp.float32)
    acc = lax.fori_loop(0, SIDE, step, (zero,) * 32)
    for r in range(4):
        column = jnp.sum(fold_rows(list(acc[r * 8 : r * 8 + 8])), axis=1, keepdims=True)
        sums = jnp.where(iota(1) == lane + r, column, sums)
    return sums


def picked(table, index):
    return jnp.take_along_axis(table, index, axis=1, mode="promise_in_bounds")


def apply_and_reduce(
    nx, ny, prev, block, seeds, levels, hop, onsite, product, stats,
    fields, seed_v, level_v, hop_v, onsite_v, table, coef_x, coef_y, coef_z, energy,
    edge_y, halo_x, halo_y, seed_edge, seed_x, seed_y, slots_one, slots_two,
    load_sem, halo_send, halo_recv, sum_send, sum_recv, store_sem,
):
    gx, gy = lax.axis_index("gx"), lax.axis_index("gy")
    right, left = ((gx + 1) % nx, gy), ((gx + nx - 1) % nx, gy)
    above, below = (gx, (gy + 1) % ny), (gx, (gy + ny - 1) % ny)
    pos = position()
    plans = [offsets(dims) for dims in STAGES]

    barrier = pltpu.get_barrier_semaphore()
    partners = [right, left, above, below]
    partners += [device(peer(pos, off)) for plan in plans for off in plan]
    for partner in partners:
        pl.semaphore_signal(barrier, inc=1, device_id=partner, device_id_type=MESH)

    inside = pl.ds(8, ROWS)
    loads = [
        pltpu.make_async_copy(seeds, seed_v, load_sem.at[0]),
        pltpu.make_async_copy(block, fields.at[:, pl.ds(WIDTH, WIDTH), inside, :], load_sem.at[1]),
        pltpu.make_async_copy(hop, hop_v, load_sem.at[2]),
        pltpu.make_async_copy(onsite, onsite_v, load_sem.at[3]),
        pltpu.make_async_copy(levels, level_v, load_sem.at[4]),
        pltpu.make_async_copy(prev, fields.at[:, pl.ds(0, WIDTH), inside, :], load_sem.at[5]),
    ]
    for load in loads:
        load.start()

    pl.semaphore_wait(barrier, len(partners))

    def send(i, src, dst, to):
        return pltpu.make_async_remote_copy(
            src_ref=src, dst_ref=dst, send_sem=halo_send.at[i], recv_sem=halo_recv.at[i],
            device_id=to, device_id_type=MESH,
        )

    last, lead = pl.ds(ROWS - 8, 8), pl.ds(0, 8)
    sends = [
        send(0, seeds.at[0, last, :], seed_x, right),
        send(1, block.at[:, :, last, :], halo_x.at[0], right),
        send(2, block.at[:, :, lead, :], halo_x.at[1], left),
    ]
    for copy in sends:
        copy.start()
    loads[0].wait()
    seed_edge[...] = seed_v[1, pl.ds(7, 8, stride=8), :]
    loads[1].wait()

    def pack(n, _):
        for orb in range(ORB):
            edge_y[0, orb, n] = fields[orb, WIDTH + n, pl.ds(15, 8, stride=8), :]
            edge_y[1, orb, n] = fields[orb, WIDTH + n, pl.ds(8, 8, stride=8), :]
        return 0

    lax.fori_loop(0, WIDTH, pack, 0)
    more = [
        send(3, seed_edge, seed_y, above),
        send(4, edge_y.at[0], halo_y.at[0], above),
        send(5, edge_y.at[1], halo_y.at[1], below),
    ]
    for copy in more:
        copy.start()
    sends += more

    for load in loads[2:5]:
        load.wait()
    zero = jnp.zeros((8, LANES), jnp.float32)

    for a in range(ORB):
        table[27 + a, :, 0:KINDS] = jnp.broadcast_to(onsite_v[a : a + 1, :], (8, KINDS))
        for d in range(3):
            for b in range(ORB):
                table[d * 9 + a * 3 + b, :, 0:KINDS] = jnp.broadcast_to(hop_v[d, a, b : b + 1, :], (8, KINDS))

    for n in range(WIDTH):
        for orb in range(ORB):
            fields[orb, WIDTH + n, 0:8, :] = zero
            fields[orb, WIDTH + n, ROWS + 8 : ROWS + 16, :] = zero
    for ab in range(9):
        coef_x[ab, 0:8, :] = zero
    inner_row = iota(0) < 7

    def look_up(x, _):
        rows = pl.ds(pl.multiple_of(8 * x, 8), 8)
        later = pl.ds(pl.multiple_of(8 * x + 8, 8), 8)
        at_x, at_y, at_z = (seed_v[d, rows, :] for d in range(3))
        level = level_v[rows, :]
        for a in range(ORB):
            energy[a, rows, :] = picked(table[27 + a], level)
            for b in range(ORB):
                ab = a * 3 + b
                coef_x[ab, later, :] = picked(table[ab], at_x)
                coef_y[ab, rows, :] = jnp.where(inner_row, picked(table[9 + ab], at_y), 0.0)
                coef_z[ab, rows, :] = picked(table[18 + ab], at_z)
        return 0

    lax.fori_loop(0, SIDE, look_up, 0)

    def own(x, _):
        before = pl.ds(pl.multiple_of(8 * x, 8), 8)
        here = pl.ds(pl.multiple_of(8 * x + 8, 8), 8)
        after = pl.ds(pl.multiple_of(8 * x + 16, 8), 8)
        cx = [coef_x[ab, here, :] for ab in range(9)]
        cm = [coef_x[ab, before, :] for ab in range(9)]
        cy = [coef_y[ab, before, :] for ab in range(9)]
        cz = [coef_z[ab, before, :] for ab in range(9)]
        ce = [energy[a, before, :] for a in range(ORB)]
        for n in range(WIDTH):
            v = [fields[b, WIDTH + n, here, :] for b in range(ORB)]
            vp = [fields[b, WIDTH + n, after, :] for b in range(ORB)]
            vm = [fields[b, WIDTH + n, before, :] for b in range(ORB)]
            vz = [pltpu.roll(u, LANES - 1, axis=1) for u in v]
            vy = [pltpu.roll(u, 7, axis=0) for u in v]
            for a in range(ORB):
                carried_z = cz[a] * v[0] + cz[3 + a] * v[1] + cz[6 + a] * v[2]
                carried_y = cy[a] * v[0] + cy[3 + a] * v[1] + cy[6 + a] * v[2]
                out = ce[a] * v[a] + pltpu.roll(carried_z, 1, axis=1) + pltpu.roll(carried_y, 1, axis=0)
                for b in range(ORB):
                    out = out + cx[a * 3 + b] * vp[b] + cm[b * 3 + a] * vm[b]
                    out = out + cz[a * 3 + b] * vz[b] + cy[a * 3 + b] * vy[b]
                fields[a, 2 * WIDTH + n, here, :] = out
        return 0

    lax.fori_loop(0, SIDE, own, 0)

    loads[5].wait()

    def basis_rows(i, sums):
        sums = inner_rows(fields, 4 * i, 0, 32 + 4 * i, sums)
        return inner_rows(fields, 4 * i, WIDTH, 48 + 4 * i, sums)

    sums = lax.fori_loop(0, 4, basis_rows, zero)

    for copy in sends:
        copy.wait_recv()
    cm = [picked(table[ab], seed_x[...]) for ab in range(9)]
    cb = [picked(table[9 + ab], seed_y[...]) for ab in range(9)]
    cf = [picked(table[9 + ab], seed_edge[...]) for ab in range(9)]
    cp = [coef_x[ab, ROWS : ROWS + 8, :] for ab in range(9)]

    def edges(n, _):
        for a in range(ORB):
            field = fields.at[a, 2 * WIDTH + n]
            low, high = field[8:16, :], field[ROWS : ROWS + 8, :]
            for b in range(ORB):
                low = low + cm[b * 3 + a] * halo_x[0, b, n]
                high = high + cp[a * 3 + b] * halo_x[1, b, n]
            field[8:16, :] = low
            field[ROWS : ROWS + 8, :] = high
            low, high = field[pl.ds(8, 8, stride=8), :], field[pl.ds(15, 8, stride=8), :]
            for b in range(ORB):
                low = low + cb[b * 3 + a] * halo_y[0, b, n]
                high = high + cf[a * 3 + b] * halo_y[1, b, n]
            field[pl.ds(8, 8, stride=8), :] = low
            field[pl.ds(15, 8, stride=8), :] = high
        return 0

    lax.fori_loop(0, WIDTH, edges, 0)
    keep = pltpu.make_async_copy(fields.at[:, pl.ds(2 * WIDTH, WIDTH), inside, :], product, store_sem)
    keep.start()

    def product_rows(i, sums):
        return inner_rows(fields, 4 * i, 2 * WIDTH, 4 * i, sums)

    sums = lax.fori_loop(0, 6, product_rows, sums)
    value = (sums + pltpu.roll(pltpu.roll(sums, 4, axis=0), 64, axis=1))[0:4, :]
    for s, (dims, plan, slots) in enumerate(zip(STAGES, plans, (slots_one, slots_two))):
        me, size = member(pos, dims), group_size(dims)
        slots[me] = value
        for off in plan:
            pltpu.make_async_remote_copy(
                src_ref=slots.at[me], dst_ref=slots.at[me], send_sem=sum_send.at[s], recv_sem=sum_recv.at[s],
                device_id=device(peer(pos, off)), device_id_type=MESH,
            ).start()
        bulk = slots.at[pl.ds(0, size - 1)]
        pltpu.make_async_copy(bulk, bulk, sum_recv.at[s]).wait()
        value = slots[0]
        for k in range(1, size):
            value = value + slots[k]
    stats[...] = value
    for copy in sends:
        copy.wait_send()
    for s, (dims, slots) in enumerate(zip(STAGES, (slots_one, slots_two))):
        bulk = slots.at[pl.ds(0, group_size(dims) - 1)]
        pltpu.make_async_copy(bulk, bulk, sum_send.at[s]).wait()
    keep.wait()


def wide(matrix):
    return jnp.concatenate([matrix, jnp.zeros((LANES - matrix.shape[0], LANES), jnp.float32)], axis=0)


def rows_dot(left, right):
    return lax.dot_general(
        left, wide(right), (((1,), (1,)), ((), ())), precision=HIGH, preferred_element_type=jnp.float32
    )


def finish(
    count, prev, block, product, stats, out, alpha, beta,
    fields, result, columns, spread, load_sem, store_sem,
):
    loads = []
    for orb in range(ORB):
        for i, source in enumerate((prev, block, product)):
            target = fields.at[orb, pl.ds(i * WIDTH, WIDTH)]
            loads.append(pltpu.make_async_copy(source.at[orb], target, load_sem.at[orb, i]))
    for load in loads:
        load.start()
    row, lane = iota(0), iota(1)
    scaled = stats[...] * (1.0 / count)
    sums = jnp.concatenate([scaled, pltpu.roll(scaled, 64, axis=1)], axis=0)
    first = jnp.where(lane < 16, sums, 0.0)
    norms = jnp.where(lane < 8, pltpu.roll(sums, LANES - 16, axis=1), 0.0)
    metric = [jnp.where(lane < 16, pltpu.roll(sums, LANES - at, axis=1), 0.0) for at in (32, 48)]
    twice = [jnp.where(row + 8 * i == lane, 2.0, 0.0) - metric[i] for i in range(2)]
    metric, twice = (jnp.concatenate(m, axis=0) for m in (metric, twice))
    coeffs = rows_dot(first, twice)
    for k in range(2 * WIDTH):
        spread[k] = jnp.broadcast_to(coeffs[:, k : k + 1], (8, LANES))
    last = jnp.where(lane < 8, pltpu.roll(first, LANES - 8, axis=1), 0.0)
    unit = jnp.where(row == lane, 1.0, 0.0)
    alpha[...] = rows_dot(unit, last)[:, 0:WIDTH]
    gram = norms + rows_dot(rows_dot(coeffs, metric) - first, coeffs) - rows_dot(coeffs, first)
    for j in range(WIDTH):
        columns[j] = jnp.broadcast_to(gram[:, j : j + 1], (8, LANES))

    a = [[jnp.broadcast_to(columns[j, i : i + 1, :], (8, LANES)) for j in range(i + 1)] for i in range(WIDTH)]
    inverse = [[None] * WIDTH for _ in range(WIDTH)]
    upper = jnp.zeros((8, LANES), jnp.float32)
    for j in range(WIDTH):
        inverse[j][j] = lax.rsqrt(a[j][j])
        for i in range(j, WIDTH):
            a[i][j] = a[i][j] * inverse[j][j]
            upper = jnp.where((row == j) & (lane == i), a[i][j], upper)
        for i in range(j + 1, WIDTH):
            for k in range(j + 1, i + 1):
                a[i][k] = a[i][k] - a[i][j] * a[k][j]
    for i in range(WIDTH):
        for j in range(i):
            total = a[i][j] * inverse[j][j]
            for k in range(j + 1, i):
                total = total + a[i][k] * inverse[k][j]
            inverse[i][j] = -(total * inverse[i][i])
    beta[...] = upper[:, 0:WIDTH]
    for i in range(WIDTH):
        for j in range(i + 1):
            columns[WIDTH + i * WIDTH + j] = inverse[i][j]

    stores = []
    for orb in range(ORB):
        for load in loads[3 * orb : 3 * orb + 3]:
            load.wait()

        def rest(m, _):
            for half in range(2):
                tiles = [pl.ds(8 * (4 * half + x), 8) for x in range(4)]
                acc = [[fields[orb, 2 * WIDTH + 2 * m + r, t, :] for t in tiles] for r in range(2)]
                for k in range(2 * WIDTH):
                    c = [jnp.broadcast_to(spread[k, pl.ds(2 * m + r, 1), :], (8, LANES)) for r in range(2)]
                    for x, t in enumerate(tiles):
                        q = fields[orb, k, t, :]
                        for r in range(2):
                            acc[r][x] = acc[r][x] - c[r] * q
                for r in range(2):
                    for x, t in enumerate(tiles):
                        fields[orb, 2 * WIDTH + 2 * m + r, t, :] = acc[r][x]
            return 0

        lax.fori_loop(0, WIDTH // 2, rest, 0)
        for n in range(WIDTH):
            acc = None
            for m in range(n + 1):
                c = columns[WIDTH + n * WIDTH + m]
                terms = [c * fields[orb, 2 * WIDTH + m, 8 * x : 8 * x + 8, :] for x in range(SIDE)]
                acc = terms if acc is None else [p + q for p, q in zip(acc, terms)]
            for x in range(SIDE):
                result[orb, n, 8 * x : 8 * x + 8, :] = acc[x]
        stores.append(pltpu.make_async_copy(result.at[orb], out.at[orb], store_sem.at[orb]))
        stores[-1].start()
    for store in stores:
        store.wait()


def per_device(nx, ny, prev, block, seeds, levels, hop, onsite):
    f32, i32 = jnp.float32, jnp.int32
    shape = block.shape
    prev, block = (v.reshape(ORB, WIDTH, ROWS, LANES) for v in (prev, block))
    hop, onsite = hop.transpose(0, 2, 3, 1), onsite.T
    seeds, levels = seeds.reshape(3, ROWS, LANES), levels.reshape(ROWS, LANES)
    hbm, vmem = pl.BlockSpec(memory_space=pltpu.HBM), pl.BlockSpec(memory_space=pltpu.VMEM)
    plane = (2, ORB, WIDTH, 8, LANES)
    dma = pltpu.SemaphoreType.DMA
    product, stats = pl.pallas_call(
        functools.partial(apply_and_reduce, nx, ny),
        out_shape=(jax.ShapeDtypeStruct(block.shape, f32), jax.ShapeDtypeStruct((4, LANES), f32)),
        in_specs=[hbm] * 6,
        out_specs=(hbm, vmem),
        scratch_shapes=[
            pltpu.VMEM((ORB, FIELDS, ROWS + 16, LANES), f32),
            pltpu.VMEM((3, ROWS, LANES), i32),
            pltpu.VMEM((ROWS, LANES), i32),
            pltpu.VMEM(hop.shape, f32),
            pltpu.VMEM(onsite.shape, f32),
            pltpu.VMEM((30, 8, LANES), f32),
            pltpu.VMEM((9, ROWS + 8, LANES), f32),
            pltpu.VMEM((9, ROWS, LANES), f32),
            pltpu.VMEM((9, ROWS, LANES), f32),
            pltpu.VMEM((ORB, ROWS, LANES), f32),
            pltpu.VMEM(plane, f32),
            pltpu.VMEM(plane, f32),
            pltpu.VMEM(plane, f32),
            pltpu.VMEM((8, LANES), i32),
            pltpu.VMEM((8, LANES), i32),
            pltpu.VMEM((8, LANES), i32),
            pltpu.VMEM((group_size(STAGES[0]), 4, LANES), f32),
            pltpu.VMEM((group_size(STAGES[1]), 4, LANES), f32),
            dma((6,)),
            dma((6,)),
            dma((6,)),
            dma((2,)),
            dma((2,)),
            dma,
        ],
        compiler_params=pltpu.CompilerParams(
            collective_id=0, has_side_effects=True, vmem_limit_bytes=58 << 20
        ),
    )(prev, block, seeds, levels, hop, onsite)
    count = float(ORB * ROWS * LANES * nx * ny)
    out, alpha, beta = pl.pallas_call(
        functools.partial(finish, count),
        out_shape=(
            jax.ShapeDtypeStruct(block.shape, f32),
            jax.ShapeDtypeStruct((WIDTH, WIDTH), f32),
            jax.ShapeDtypeStruct((WIDTH, WIDTH), f32),
        ),
        in_specs=[hbm, hbm, hbm, vmem],
        out_specs=(hbm, vmem, vmem),
        scratch_shapes=[
            pltpu.VMEM((ORB, FIELDS, ROWS, LANES), f32),
            pltpu.VMEM((ORB, WIDTH, ROWS, LANES), f32),
            pltpu.VMEM((WIDTH + WIDTH * WIDTH, 8, LANES), f32),
            pltpu.VMEM((2 * WIDTH, 8, LANES), f32),
            dma((ORB, 3)),
            dma((ORB,)),
        ],
        compiler_params=pltpu.CompilerParams(vmem_limit_bytes=58 << 20),
    )(prev, block, product, stats)
    return out.reshape(shape), alpha, beta


def solution(mesh):
    fields = P(None, None, "gx", "gy", None)
    return jax.shard_map(
        functools.partial(per_device, mesh.shape["gx"], mesh.shape["gy"]),
        mesh=mesh,
        in_specs=(fields, fields, P(None, "gx", "gy", None), P("gx", "gy", None), P(), P()),
        out_specs=(fields, P(), P()),
        check_vma=False,
    )
```

```python
import functools

import jax
import jax.numpy as jnp
from jax import lax
from jax.experimental import pallas as pl
from jax.experimental.pallas import tpu as pltpu
from jax.sharding import PartitionSpec as P

HIGH = lax.Precision.HIGHEST
MESH = pl.DeviceIdType.MESH
ORB, WIDTH, SIDE, LANES, KINDS = 3, 8, 8, 128, 16
ROWS = SIDE * SIDE
FIELDS = 3 * WIDTH

DIGITS = {"x": 4, "zh": 4, "y": 8, "zl": 2, "core": 2}
STAGES = (("core", "y"), ("x", "zh", "zl"))


def position():
    gx, gy = lax.axis_index("gx"), lax.axis_index("gy")
    return {"x": gx // 4, "zh": gx % 4, "y": gy // 4, "zl": (gy // 2) % 2, "core": gy % 2}


def device(pos):
    return (pos["x"] * 4 + pos["zh"], pos["y"] * 4 + pos["zl"] * 2 + pos["core"])


def group_size(dims):
    size = 1
    for dim in dims:
        size *= DIGITS[dim]
    return size


def member(pos, dims):
    index = 0
    for dim in dims:
        index = index * DIGITS[dim] + pos[dim]
    return index


def offsets(dims):
    found = []
    for k in range(1, group_size(dims)):
        off, rest = {}, k
        for dim in reversed(dims):
            off[dim] = rest % DIGITS[dim]
            rest //= DIGITS[dim]
        hops = 0
        if "y" in off:
            hops += min(off["y"], 8 - off["y"])
        if "x" in off:
            hops += min(off["x"], 4 - off["x"])
        if "zh" in off:
            z = (off["zh"] * 2 + off.get("zl", 0)) % 8
            hops += min(z, 8 - z)
        found.append((-hops, k, off))
    return [off for _, _, off in sorted(found, key=lambda t: t[:2])]


def moved(pos, dim, steps):
    new = dict(pos)
    if dim == "z":
        z = (pos["zh"] * 2 + pos["zl"] + steps) % 8
        new["zh"], new["zl"] = z // 2, z % 2
    else:
        new[dim] = (pos[dim] + steps) % DIGITS[dim]
    return device(new)


def peer(pos, off):
    return {d: (pos[d] + off[d]) % DIGITS[d] if off.get(d) else pos[d] for d in pos}


def iota(axis):
    return lax.broadcasted_iota(jnp.int32, (8, LANES), axis)


def fold_rows(parts):
    row = iota(0)
    for bit in (1, 2, 4):
        low = (row & bit) == 0
        parts = [
            jnp.where(low, a, b) + pltpu.roll(jnp.where(low, b, a), bit, axis=0)
            for a, b in zip(parts[0::2], parts[1::2])
        ]
    return parts[0]


def products(fields, first, others, planes, acc):
    for x in planes:
        rows = pl.ds(8 * x + 8, 8) if isinstance(x, int) else pl.ds(pl.multiple_of(8 * x + 8, 8), 8)
        for orb in range(ORB):
            left = [fields[orb, first + r, rows, :] for r in range(4)]
            right = [fields[orb, others + s, rows, :] for s in range(8)]
            acc = [acc[r * 8 + s] + left[r] * right[s] for r in range(4) for s in range(8)]
    return acc


def inner_rows(fields, first, others, lane, sums):
    zero = jnp.zeros((8, LANES), jnp.float32)
    acc = lax.fori_loop(0, SIDE, lambda x, acc: tuple(products(fields, first, others, (x,), acc)), (zero,) * 32)
    for r in range(4):
        column = jnp.sum(fold_rows(list(acc[r * 8 : r * 8 + 8])), axis=1, keepdims=True)
        sums = jnp.where(iota(1) == lane + r, column, sums)
    return sums


def picked(table, index):
    return jnp.take_along_axis(table, index, axis=1, mode="promise_in_bounds")


def apply_and_reduce(
    nx, ny, prev, block, seeds, levels, hop, onsite, product, stats,
    fields, seed_v, level_v, hop_v, onsite_v, table, coef_x, coef_y, coef_z, energy,
    edge_y, halo_x, halo_y, seed_edge, seed_x, seed_y, slots_one, slots_two, partial, folded,
    load_sem, halo_send, halo_recv, sum_send, sum_recv, store_sem, known,
):
    gx, gy = lax.axis_index("gx"), lax.axis_index("gy")
    right, left = ((gx + 1) % nx, gy), ((gx + nx - 1) % nx, gy)
    above, below = (gx, (gy + 1) % ny), (gx, (gy + ny - 1) % ny)
    pos = position()
    plans = [offsets(dims) for dims in STAGES]

    barrier = pltpu.get_barrier_semaphore()
    rings = [moved(pos, dim, k) for dim in ("z", "y") for k in (1, -1, 2, -2)]
    across = [moved(pos, "x", k) for k in (1, 2, 3)] + [moved(pos, "core", 1)]
    partners = [right, left, above, below] + rings + across

    def greet(sem, devices):
        for other in devices:
            pl.semaphore_signal(sem, inc=1, device_id=other, device_id_type=MESH)

    greet(barrier, partners)

    inside = pl.ds(8, ROWS)
    loads = [
        pltpu.make_async_copy(seeds, seed_v, load_sem.at[0]),
        pltpu.make_async_copy(block, fields.at[:, pl.ds(WIDTH, WIDTH), inside, :], load_sem.at[1]),
        pltpu.make_async_copy(hop, hop_v, load_sem.at[2]),
        pltpu.make_async_copy(onsite, onsite_v, load_sem.at[3]),
        pltpu.make_async_copy(levels, level_v, load_sem.at[4]),
        pltpu.make_async_copy(prev, fields.at[:, pl.ds(0, WIDTH), inside, :], load_sem.at[5]),
    ]
    for load in loads:
        load.start()

    pl.semaphore_wait(barrier, len(partners))
    greet(known.at[0], rings)

    def send(i, src, dst, to):
        return pltpu.make_async_remote_copy(
            src_ref=src, dst_ref=dst, send_sem=halo_send.at[i], recv_sem=halo_recv.at[i],
            device_id=to, device_id_type=MESH,
        )

    last, lead = pl.ds(ROWS - 8, 8), pl.ds(0, 8)
    sends = [
        send(0, seeds.at[0, last, :], seed_x, right),
        send(1, block.at[:, :, last, :], halo_x.at[0], right),
        send(2, block.at[:, :, lead, :], halo_x.at[1], left),
    ]
    for copy in sends:
        copy.start()
    loads[0].wait()
    seed_edge[...] = seed_v[1, pl.ds(7, 8, stride=8), :]
    loads[1].wait()

    def pack(n, _):
        for orb in range(ORB):
            edge_y[0, orb, n] = fields[orb, WIDTH + n, pl.ds(15, 8, stride=8), :]
            edge_y[1, orb, n] = fields[orb, WIDTH + n, pl.ds(8, 8, stride=8), :]
        return 0

    lax.fori_loop(0, WIDTH, pack, 0)
    more = [
        send(3, seed_edge, seed_y, above),
        send(4, edge_y.at[0], halo_y.at[0], above),
        send(5, edge_y.at[1], halo_y.at[1], below),
    ]
    for copy in more:
        copy.start()
    sends += more
    pl.semaphore_wait(known.at[0], len(rings))
    greet(known.at[1], across)

    for load in loads[2:5]:
        load.wait()
    zero = jnp.zeros((8, LANES), jnp.float32)

    for a in range(ORB):
        table[27 + a, :, 0:KINDS] = jnp.broadcast_to(onsite_v[a : a + 1, :], (8, KINDS))
        for d in range(3):
            for b in range(ORB):
                table[d * 9 + a * 3 + b, :, 0:KINDS] = jnp.broadcast_to(hop_v[d, a, b : b + 1, :], (8, KINDS))

    for n in range(WIDTH):
        for orb in range(ORB):
            fields[orb, WIDTH + n, 0:8, :] = zero
            fields[orb, WIDTH + n, ROWS + 8 : ROWS + 16, :] = zero
    for ab in range(9):
        coef_x[ab, 0:8, :] = zero
    inner_row = iota(0) < 7

    def look_up(x, _):
        rows = pl.ds(pl.multiple_of(8 * x, 8), 8)
        later = pl.ds(pl.multiple_of(8 * x + 8, 8), 8)
        at_x, at_y, at_z = (seed_v[d, rows, :] for d in range(3))
        level = level_v[rows, :]
        for a in range(ORB):
            energy[a, rows, :] = picked(table[27 + a], level)
            for b in range(ORB):
                ab = a * 3 + b
                coef_x[ab, later, :] = picked(table[ab], at_x)
                coef_y[ab, rows, :] = jnp.where(inner_row, picked(table[9 + ab], at_y), 0.0)
                coef_z[ab, rows, :] = picked(table[18 + ab], at_z)
        return 0

    lax.fori_loop(0, SIDE, look_up, 0)

    def own(x, _):
        before = pl.ds(pl.multiple_of(8 * x, 8), 8)
        here = pl.ds(pl.multiple_of(8 * x + 8, 8), 8)
        after = pl.ds(pl.multiple_of(8 * x + 16, 8), 8)
        cx = [coef_x[ab, here, :] for ab in range(9)]
        cm = [coef_x[ab, before, :] for ab in range(9)]
        cy = [coef_y[ab, before, :] for ab in range(9)]
        cz = [coef_z[ab, before, :] for ab in range(9)]
        ce = [energy[a, before, :] for a in range(ORB)]
        for n in range(WIDTH):
            v = [fields[b, WIDTH + n, here, :] for b in range(ORB)]
            vp = [fields[b, WIDTH + n, after, :] for b in range(ORB)]
            vm = [fields[b, WIDTH + n, before, :] for b in range(ORB)]
            vz = [pltpu.roll(u, LANES - 1, axis=1) for u in v]
            vy = [pltpu.roll(u, 7, axis=0) for u in v]
            for a in range(ORB):
                carried_z = cz[a] * v[0] + cz[3 + a] * v[1] + cz[6 + a] * v[2]
                carried_y = cy[a] * v[0] + cy[3 + a] * v[1] + cy[6 + a] * v[2]
                out = ce[a] * v[a] + pltpu.roll(carried_z, 1, axis=1) + pltpu.roll(carried_y, 1, axis=0)
                for b in range(ORB):
                    out = out + cx[a * 3 + b] * vp[b] + cm[b * 3 + a] * vm[b]
                    out = out + cz[a * 3 + b] * vz[b] + cy[a * 3 + b] * vy[b]
                fields[a, 2 * WIDTH + n, here, :] = out
        return 0

    lax.fori_loop(0, SIDE, own, 0)

    loads[5].wait()

    def basis_rows(i, sums):
        sums = inner_rows(fields, 4 * i, 0, 32 + 4 * i, sums)
        return inner_rows(fields, 4 * i, WIDTH, 48 + 4 * i, sums)

    sums = lax.fori_loop(0, 4, basis_rows, zero)

    for i in (3, 4, 5):
        sends[i].wait_recv()
    cb = [picked(table[9 + ab], seed_y[...]) for ab in range(9)]
    cf = [picked(table[9 + ab], seed_edge[...]) for ab in range(9)]

    def edges_y(n, _):
        for a in range(ORB):
            field = fields.at[a, 2 * WIDTH + n]
            low, high = field[pl.ds(8, 8, stride=8), :], field[pl.ds(15, 8, stride=8), :]
            for b in range(ORB):
                low = low + cb[b * 3 + a] * halo_y[0, b, n]
                high = high + cf[a * 3 + b] * halo_y[1, b, n]
            field[pl.ds(8, 8, stride=8), :] = low
            field[pl.ds(15, 8, stride=8), :] = high
        return 0

    lax.fori_loop(0, WIDTH, edges_y, 0)

    def inner_planes(i, _):
        acc = lax.fori_loop(
            1, SIDE - 1, lambda x, acc: tuple(products(fields, 4 * i, 2 * WIDTH, (x,), acc)), (zero,) * 32
        )
        for k in range(32):
            partial[i, k] = acc[k]
        return 0

    lax.fori_loop(0, 6, inner_planes, 0)

    for i in (0, 1, 2):
        sends[i].wait_recv()
    cm = [picked(table[ab], seed_x[...]) for ab in range(9)]
    cp = [coef_x[ab, ROWS : ROWS + 8, :] for ab in range(9)]

    def edges_x(n, _):
        for a in range(ORB):
            field = fields.at[a, 2 * WIDTH + n]
            low, high = field[8:16, :], field[ROWS : ROWS + 8, :]
            for b in range(ORB):
                low = low + cm[b * 3 + a] * halo_x[0, b, n]
                high = high + cp[a * 3 + b] * halo_x[1, b, n]
            field[8:16, :] = low
            field[ROWS : ROWS + 8, :] = high
        return 0

    lax.fori_loop(0, WIDTH, edges_x, 0)
    keep = pltpu.make_async_copy(fields.at[:, pl.ds(2 * WIDTH, WIDTH), inside, :], product, store_sem)
    keep.start()

    def outer_planes(i, _):
        acc = products(fields, 4 * i, 2 * WIDTH, (0, SIDE - 1), [partial[i, k] for k in range(32)])
        for r in range(4):
            folded[4 * i + r] = fold_rows(acc[r * 8 : r * 8 + 8])
        return 0

    lax.fori_loop(0, 6, outer_planes, 0)
    for k in range(FIELDS):
        sums = jnp.where(iota(1) == k, jnp.sum(folded[k], axis=1, keepdims=True), sums)
    value = (sums + pltpu.roll(pltpu.roll(sums, 4, axis=0), 64, axis=1))[0:4, :]
    pl.semaphore_wait(known.at[1], len(across))
    for s, (dims, plan, slots) in enumerate(zip(STAGES, plans, (slots_one, slots_two))):
        me, size = member(pos, dims), group_size(dims)
        slots[me] = value
        for off in plan:
            pltpu.make_async_remote_copy(
                src_ref=slots.at[me], dst_ref=slots.at[me], send_sem=sum_send.at[s], recv_sem=sum_recv.at[s],
                device_id=device(peer(pos, off)), device_id_type=MESH,
            ).start()
        bulk = slots.at[pl.ds(0, size - 1)]
        pltpu.make_async_copy(bulk, bulk, sum_recv.at[s]).wait()
        value = slots[0]
        for k in range(1, size):
            value = value + slots[k]
    stats[...] = value
    for copy in sends:
        copy.wait_send()
    for s, (dims, slots) in enumerate(zip(STAGES, (slots_one, slots_two))):
        bulk = slots.at[pl.ds(0, group_size(dims) - 1)]
        pltpu.make_async_copy(bulk, bulk, sum_send.at[s]).wait()
    keep.wait()


def wide(matrix):
    return jnp.concatenate([matrix, jnp.zeros((LANES - matrix.shape[0], LANES), jnp.float32)], axis=0)


def rows_dot(left, right):
    return lax.dot_general(
        left, wide(right), (((1,), (1,)), ((), ())), precision=HIGH, preferred_element_type=jnp.float32
    )


def finish(
    count, prev, block, product, stats, out, alpha, beta,
    fields, result, columns, spread, load_sem, store_sem,
):
    loads = []
    for orb in range(ORB):
        for i, source in enumerate((prev, block, product)):
            target = fields.at[orb, pl.ds(i * WIDTH, WIDTH)]
            loads.append(pltpu.make_async_copy(source.at[orb], target, load_sem.at[orb, i]))
    for load in loads:
        load.start()
    row, lane = iota(0), iota(1)
    scaled = stats[...] * (1.0 / count)
    sums = jnp.concatenate([scaled, pltpu.roll(scaled, 64, axis=1)], axis=0)
    first = jnp.where(lane < 16, sums, 0.0)
    norms = jnp.where(lane < 8, pltpu.roll(sums, LANES - 16, axis=1), 0.0)
    metric = [jnp.where(lane < 16, pltpu.roll(sums, LANES - at, axis=1), 0.0) for at in (32, 48)]
    twice = [jnp.where(row + 8 * i == lane, 2.0, 0.0) - metric[i] for i in range(2)]
    metric, twice = (jnp.concatenate(m, axis=0) for m in (metric, twice))
    coeffs = rows_dot(first, twice)
    for k in range(2 * WIDTH):
        spread[k] = jnp.broadcast_to(coeffs[:, k : k + 1], (8, LANES))
    last = jnp.where(lane < 8, pltpu.roll(first, LANES - 8, axis=1), 0.0)
    unit = jnp.where(row == lane, 1.0, 0.0)
    alpha[...] = rows_dot(unit, last)[:, 0:WIDTH]
    gram = norms + rows_dot(rows_dot(coeffs, metric) - first, coeffs) - rows_dot(coeffs, first)
    for j in range(WIDTH):
        columns[j] = jnp.broadcast_to(gram[:, j : j + 1], (8, LANES))

    a = [[jnp.broadcast_to(columns[j, i : i + 1, :], (8, LANES)) for j in range(i + 1)] for i in range(WIDTH)]
    inverse = [[None] * WIDTH for _ in range(WIDTH)]
    upper = jnp.zeros((8, LANES), jnp.float32)
    for j in range(WIDTH):
        inverse[j][j] = lax.rsqrt(a[j][j])
        for i in range(j, WIDTH):
            a[i][j] = a[i][j] * inverse[j][j]
            upper = jnp.where((row == j) & (lane == i), a[i][j], upper)
        for i in range(j + 1, WIDTH):
            for k in range(j + 1, i + 1):
                a[i][k] = a[i][k] - a[i][j] * a[k][j]
    for i in range(WIDTH):
        for j in range(i):
            total = a[i][j] * inverse[j][j]
            for k in range(j + 1, i):
                total = total + a[i][k] * inverse[k][j]
            inverse[i][j] = -(total * inverse[i][i])
    beta[...] = upper[:, 0:WIDTH]
    for i in range(WIDTH):
        for j in range(i + 1):
            columns[WIDTH + i * WIDTH + j] = inverse[i][j]

    stores = []
    for orb in range(ORB):
        for load in loads[3 * orb : 3 * orb + 3]:
            load.wait()

        def rest(m, _):
            for half in range(2):
                tiles = [pl.ds(8 * (4 * half + x), 8) for x in range(4)]
                acc = [[fields[orb, 2 * WIDTH + 2 * m + r, t, :] for t in tiles] for r in range(2)]
                for k in range(2 * WIDTH):
                    c = [jnp.broadcast_to(spread[k, pl.ds(2 * m + r, 1), :], (8, LANES)) for r in range(2)]
                    for x, t in enumerate(tiles):
                        q = fields[orb, k, t, :]
                        for r in range(2):
                            acc[r][x] = acc[r][x] - c[r] * q
                for r in range(2):
                    for x, t in enumerate(tiles):
                        fields[orb, 2 * WIDTH + 2 * m + r, t, :] = acc[r][x]
            return 0

        lax.fori_loop(0, WIDTH // 2, rest, 0)
        for n in range(WIDTH):
            acc = None
            for m in range(n + 1):
                c = columns[WIDTH + n * WIDTH + m]
                terms = [c * fields[orb, 2 * WIDTH + m, 8 * x : 8 * x + 8, :] for x in range(SIDE)]
                acc = terms if acc is None else [p + q for p, q in zip(acc, terms)]
            for x in range(SIDE):
                result[orb, n, 8 * x : 8 * x + 8, :] = acc[x]
        stores.append(pltpu.make_async_copy(result.at[orb], out.at[orb], store_sem.at[orb]))
        stores[-1].start()
    for store in stores:
        store.wait()


def per_device(nx, ny, prev, block, seeds, levels, hop, onsite):
    f32, i32 = jnp.float32, jnp.int32
    shape = block.shape
    prev, block = (v.reshape(ORB, WIDTH, ROWS, LANES) for v in (prev, block))
    hop, onsite = hop.transpose(0, 2, 3, 1), onsite.T
    seeds, levels = seeds.reshape(3, ROWS, LANES), levels.reshape(ROWS, LANES)
    hbm, vmem = pl.BlockSpec(memory_space=pltpu.HBM), pl.BlockSpec(memory_space=pltpu.VMEM)
    plane = (2, ORB, WIDTH, 8, LANES)
    dma = pltpu.SemaphoreType.DMA
    product, stats = pl.pallas_call(
        functools.partial(apply_and_reduce, nx, ny),
        out_shape=(jax.ShapeDtypeStruct(block.shape, f32), jax.ShapeDtypeStruct((4, LANES), f32)),
        in_specs=[hbm] * 6,
        out_specs=(hbm, vmem),
        scratch_shapes=[
            pltpu.VMEM((ORB, FIELDS, ROWS + 16, LANES), f32),
            pltpu.VMEM((3, ROWS, LANES), i32),
            pltpu.VMEM((ROWS, LANES), i32),
            pltpu.VMEM(hop.shape, f32),
            pltpu.VMEM(onsite.shape, f32),
            pltpu.VMEM((30, 8, LANES), f32),
            pltpu.VMEM((9, ROWS + 8, LANES), f32),
            pltpu.VMEM((9, ROWS, LANES), f32),
            pltpu.VMEM((9, ROWS, LANES), f32),
            pltpu.VMEM((ORB, ROWS, LANES), f32),
            pltpu.VMEM(plane, f32),
            pltpu.VMEM(plane, f32),
            pltpu.VMEM(plane, f32),
            pltpu.VMEM((8, LANES), i32),
            pltpu.VMEM((8, LANES), i32),
            pltpu.VMEM((8, LANES), i32),
            pltpu.VMEM((group_size(STAGES[0]), 4, LANES), f32),
            pltpu.VMEM((group_size(STAGES[1]), 4, LANES), f32),
            pltpu.VMEM((6, 32, 8, LANES), f32),
            pltpu.VMEM((FIELDS, 8, LANES), f32),
            dma((6,)),
            dma((6,)),
            dma((6,)),
            dma((2,)),
            dma((2,)),
            dma,
            pltpu.SemaphoreType.REGULAR((2,)),
        ],
        compiler_params=pltpu.CompilerParams(
            collective_id=0, has_side_effects=True, vmem_limit_bytes=58 << 20
        ),
    )(prev, block, seeds, levels, hop, onsite)
    count = float(ORB * ROWS * LANES * nx * ny)
    out, alpha, beta = pl.pallas_call(
        functools.partial(finish, count),
        out_shape=(
            jax.ShapeDtypeStruct(block.shape, f32),
            jax.ShapeDtypeStruct((WIDTH, WIDTH), f32),
            jax.ShapeDtypeStruct((WIDTH, WIDTH), f32),
        ),
        in_specs=[hbm, hbm, hbm, vmem],
        out_specs=(hbm, vmem, vmem),
        scratch_shapes=[
            pltpu.VMEM((ORB, FIELDS, ROWS, LANES), f32),
            pltpu.VMEM((ORB, WIDTH, ROWS, LANES), f32),
            pltpu.VMEM((WIDTH + WIDTH * WIDTH, 8, LANES), f32),
            pltpu.VMEM((2 * WIDTH, 8, LANES), f32),
            dma((ORB, 3)),
            dma((ORB,)),
        ],
        compiler_params=pltpu.CompilerParams(vmem_limit_bytes=58 << 20),
    )(prev, block, product, stats)
    return out.reshape(shape), alpha, beta


def solution(mesh):
    fields = P(None, None, "gx", "gy", None)
    return jax.shard_map(
        functools.partial(per_device, mesh.shape["gx"], mesh.shape["gy"]),
        mesh=mesh,
        in_specs=(fields, fields, P(None, "gx", "gy", None), P("gx", "gy", None), P(), P()),
        out_specs=(fields, P(), P()),
        check_vma=False,
    )
```

```python
import functools

import jax
import jax.numpy as jnp
from jax import lax
from jax.experimental import pallas as pl
from jax.experimental.pallas import tpu as pltpu
from jax.sharding import PartitionSpec as P

HIGH = lax.Precision.HIGHEST
MESH = pl.DeviceIdType.MESH
ORB, WIDTH, SIDE, LANES, KINDS = 3, 8, 8, 128, 16
ROWS = SIDE * SIDE
FIELDS = 3 * WIDTH

DIGITS = {"x": 4, "zh": 4, "y": 8, "zl": 2, "core": 2}
STAGES = (("core", "y"), ("x", "zh", "zl"))


def position():
    gx, gy = lax.axis_index("gx"), lax.axis_index("gy")
    return {"x": gx // 4, "zh": gx % 4, "y": gy // 4, "zl": (gy // 2) % 2, "core": gy % 2}


def device(pos):
    return (pos["x"] * 4 + pos["zh"], pos["y"] * 4 + pos["zl"] * 2 + pos["core"])


def group_size(dims):
    size = 1
    for dim in dims:
        size *= DIGITS[dim]
    return size


def member(pos, dims):
    index = 0
    for dim in dims:
        index = index * DIGITS[dim] + pos[dim]
    return index


def offsets(dims):
    found = []
    for k in range(1, group_size(dims)):
        off, rest = {}, k
        for dim in reversed(dims):
            off[dim] = rest % DIGITS[dim]
            rest //= DIGITS[dim]
        hops = 0
        if "y" in off:
            hops += min(off["y"], 8 - off["y"])
        if "x" in off:
            hops += min(off["x"], 4 - off["x"])
        if "zh" in off:
            z = (off["zh"] * 2 + off.get("zl", 0)) % 8
            hops += min(z, 8 - z)
        found.append((-hops, k, off))
    return [off for _, _, off in sorted(found, key=lambda t: t[:2])]


def moved(pos, dim, steps):
    new = dict(pos)
    if dim == "z":
        z = (pos["zh"] * 2 + pos["zl"] + steps) % 8
        new["zh"], new["zl"] = z // 2, z % 2
    else:
        new[dim] = (pos[dim] + steps) % DIGITS[dim]
    return device(new)


def peer(pos, off):
    return {d: (pos[d] + off[d]) % DIGITS[d] if off.get(d) else pos[d] for d in pos}


def iota(axis):
    return lax.broadcasted_iota(jnp.int32, (8, LANES), axis)


def fold_rows(parts):
    row = iota(0)
    for bit in (1, 2, 4):
        low = (row & bit) == 0
        parts = [
            jnp.where(low, a, b) + pltpu.roll(jnp.where(low, b, a), bit, axis=0)
            for a, b in zip(parts[0::2], parts[1::2])
        ]
    return parts[0]


def products(fields, first, others, planes, acc):
    for x in planes:
        rows = pl.ds(8 * x + 8, 8) if isinstance(x, int) else pl.ds(pl.multiple_of(8 * x + 8, 8), 8)
        for orb in range(ORB):
            left = [fields[orb, first + r, rows, :] for r in range(4)]
            right = [fields[orb, others + s, rows, :] for s in range(8)]
            acc = [acc[r * 8 + s] + left[r] * right[s] for r in range(4) for s in range(8)]
    return acc


def inner_rows(fields, first, others, lane, sums):
    zero = jnp.zeros((8, LANES), jnp.float32)
    acc = lax.fori_loop(0, SIDE, lambda x, acc: tuple(products(fields, first, others, (x,), acc)), (zero,) * 32)
    for r in range(4):
        column = jnp.sum(fold_rows(list(acc[r * 8 : r * 8 + 8])), axis=1, keepdims=True)
        sums = jnp.where(iota(1) == lane + r, column, sums)
    return sums


def picked(table, index):
    return jnp.take_along_axis(table, index, axis=1, mode="promise_in_bounds")


def apply_and_reduce(
    nx, ny, prev, block, seeds, levels, hop, onsite, fields, stats,
    seed_v, level_v, hop_v, onsite_v, table, coef_x, coef_y, coef_z, energy,
    edge_y, halo_x, halo_y, seed_edge, seed_x, seed_y, slots_one, slots_two, partial, folded,
    load_sem, halo_send, halo_recv, sum_send, sum_recv, known,
):
    gx, gy = lax.axis_index("gx"), lax.axis_index("gy")
    right, left = ((gx + 1) % nx, gy), ((gx + nx - 1) % nx, gy)
    above, below = (gx, (gy + 1) % ny), (gx, (gy + ny - 1) % ny)
    pos = position()
    plans = [offsets(dims) for dims in STAGES]

    barrier = pltpu.get_barrier_semaphore()
    rings = [moved(pos, dim, k) for dim in ("z", "y") for k in (1, -1, 2, -2)]
    across = [moved(pos, "x", k) for k in (1, 2, 3)] + [moved(pos, "core", 1)]
    partners = [right, left, above, below] + rings + across

    def greet(sem, devices):
        for other in devices:
            pl.semaphore_signal(sem, inc=1, device_id=other, device_id_type=MESH)

    greet(barrier, partners)

    inside = pl.ds(8, ROWS)
    loads = [
        pltpu.make_async_copy(seeds, seed_v, load_sem.at[0]),
        pltpu.make_async_copy(block, fields.at[:, pl.ds(WIDTH, WIDTH), inside, :], load_sem.at[1]),
        pltpu.make_async_copy(hop, hop_v, load_sem.at[2]),
        pltpu.make_async_copy(onsite, onsite_v, load_sem.at[3]),
        pltpu.make_async_copy(levels, level_v, load_sem.at[4]),
        pltpu.make_async_copy(prev, fields.at[:, pl.ds(0, WIDTH), inside, :], load_sem.at[5]),
    ]
    for load in loads:
        load.start()

    pl.semaphore_wait(barrier, len(partners))
    greet(known.at[0], rings)

    def send(i, src, dst, to):
        return pltpu.make_async_remote_copy(
            src_ref=src, dst_ref=dst, send_sem=halo_send.at[i], recv_sem=halo_recv.at[i],
            device_id=to, device_id_type=MESH,
        )

    last, lead = pl.ds(ROWS - 8, 8), pl.ds(0, 8)
    sends = [
        send(0, seeds.at[0, last, :], seed_x, right),
        send(1, block.at[:, :, last, :], halo_x.at[0], right),
        send(2, block.at[:, :, lead, :], halo_x.at[1], left),
    ]
    for copy in sends:
        copy.start()
    loads[0].wait()
    seed_edge[...] = seed_v[1, pl.ds(7, 8, stride=8), :]
    loads[1].wait()

    def pack(n, _):
        for orb in range(ORB):
            edge_y[0, orb, n] = fields[orb, WIDTH + n, pl.ds(15, 8, stride=8), :]
            edge_y[1, orb, n] = fields[orb, WIDTH + n, pl.ds(8, 8, stride=8), :]
        return 0

    lax.fori_loop(0, WIDTH, pack, 0)
    more = [
        send(3, seed_edge, seed_y, above),
        send(4, edge_y.at[0], halo_y.at[0], above),
        send(5, edge_y.at[1], halo_y.at[1], below),
    ]
    for copy in more:
        copy.start()
    sends += more
    pl.semaphore_wait(known.at[0], len(rings))
    greet(known.at[1], across)

    for load in loads[2:5]:
        load.wait()
    zero = jnp.zeros((8, LANES), jnp.float32)

    for a in range(ORB):
        table[27 + a, :, 0:KINDS] = jnp.broadcast_to(onsite_v[a : a + 1, :], (8, KINDS))
        for d in range(3):
            for b in range(ORB):
                table[d * 9 + a * 3 + b, :, 0:KINDS] = jnp.broadcast_to(hop_v[d, a, b : b + 1, :], (8, KINDS))

    for n in range(WIDTH):
        for orb in range(ORB):
            fields[orb, WIDTH + n, 0:8, :] = zero
            fields[orb, WIDTH + n, ROWS + 8 : ROWS + 16, :] = zero
    for ab in range(9):
        coef_x[ab, 0:8, :] = zero
    inner_row = iota(0) < 7

    def look_up(x, _):
        rows = pl.ds(pl.multiple_of(8 * x, 8), 8)
        later = pl.ds(pl.multiple_of(8 * x + 8, 8), 8)
        at_x, at_y, at_z = (seed_v[d, rows, :] for d in range(3))
        level = level_v[rows, :]
        for a in range(ORB):
            energy[a, rows, :] = picked(table[27 + a], level)
            for b in range(ORB):
                ab = a * 3 + b
                coef_x[ab, later, :] = picked(table[ab], at_x)
                coef_y[ab, rows, :] = jnp.where(inner_row, picked(table[9 + ab], at_y), 0.0)
                coef_z[ab, rows, :] = picked(table[18 + ab], at_z)
        return 0

    lax.fori_loop(0, SIDE, look_up, 0)

    def own(x, _):
        before = pl.ds(pl.multiple_of(8 * x, 8), 8)
        here = pl.ds(pl.multiple_of(8 * x + 8, 8), 8)
        after = pl.ds(pl.multiple_of(8 * x + 16, 8), 8)
        cx = [coef_x[ab, here, :] for ab in range(9)]
        cm = [coef_x[ab, before, :] for ab in range(9)]
        cy = [coef_y[ab, before, :] for ab in range(9)]
        cz = [coef_z[ab, before, :] for ab in range(9)]
        ce = [energy[a, before, :] for a in range(ORB)]
        for n in range(WIDTH):
            v = [fields[b, WIDTH + n, here, :] for b in range(ORB)]
            vp = [fields[b, WIDTH + n, after, :] for b in range(ORB)]
            vm = [fields[b, WIDTH + n, before, :] for b in range(ORB)]
            vz = [pltpu.roll(u, LANES - 1, axis=1) for u in v]
            vy = [pltpu.roll(u, 7, axis=0) for u in v]
            for a in range(ORB):
                carried_z = cz[a] * v[0] + cz[3 + a] * v[1] + cz[6 + a] * v[2]
                carried_y = cy[a] * v[0] + cy[3 + a] * v[1] + cy[6 + a] * v[2]
                out = ce[a] * v[a] + pltpu.roll(carried_z, 1, axis=1) + pltpu.roll(carried_y, 1, axis=0)
                for b in range(ORB):
                    out = out + cx[a * 3 + b] * vp[b] + cm[b * 3 + a] * vm[b]
                    out = out + cz[a * 3 + b] * vz[b] + cy[a * 3 + b] * vy[b]
                fields[a, 2 * WIDTH + n, here, :] = out
        return 0

    lax.fori_loop(0, SIDE, own, 0)

    loads[5].wait()

    def basis_rows(i, sums):
        sums = inner_rows(fields, 4 * i, 0, 32 + 4 * i, sums)
        return inner_rows(fields, 4 * i, WIDTH, 48 + 4 * i, sums)

    sums = lax.fori_loop(0, 4, basis_rows, zero)

    for i in (3, 4, 5):
        sends[i].wait_recv()
    cb = [picked(table[9 + ab], seed_y[...]) for ab in range(9)]
    cf = [picked(table[9 + ab], seed_edge[...]) for ab in range(9)]

    def edges_y(n, _):
        for a in range(ORB):
            field = fields.at[a, 2 * WIDTH + n]
            low, high = field[pl.ds(8, 8, stride=8), :], field[pl.ds(15, 8, stride=8), :]
            for b in range(ORB):
                low = low + cb[b * 3 + a] * halo_y[0, b, n]
                high = high + cf[a * 3 + b] * halo_y[1, b, n]
            field[pl.ds(8, 8, stride=8), :] = low
            field[pl.ds(15, 8, stride=8), :] = high
        return 0

    lax.fori_loop(0, WIDTH, edges_y, 0)

    def inner_planes(i, _):
        acc = lax.fori_loop(
            1, SIDE - 1, lambda x, acc: tuple(products(fields, 4 * i, 2 * WIDTH, (x,), acc)), (zero,) * 32
        )
        for k in range(32):
            partial[i, k] = acc[k]
        return 0

    lax.fori_loop(0, 6, inner_planes, 0)

    for i in (0, 1, 2):
        sends[i].wait_recv()
    cm = [picked(table[ab], seed_x[...]) for ab in range(9)]
    cp = [coef_x[ab, ROWS : ROWS + 8, :] for ab in range(9)]

    def edges_x(n, _):
        for a in range(ORB):
            field = fields.at[a, 2 * WIDTH + n]
            low, high = field[8:16, :], field[ROWS : ROWS + 8, :]
            for b in range(ORB):
                low = low + cm[b * 3 + a] * halo_x[0, b, n]
                high = high + cp[a * 3 + b] * halo_x[1, b, n]
            field[8:16, :] = low
            field[ROWS : ROWS + 8, :] = high
        return 0

    lax.fori_loop(0, WIDTH, edges_x, 0)

    def outer_planes(i, _):
        acc = products(fields, 4 * i, 2 * WIDTH, (0, SIDE - 1), [partial[i, k] for k in range(32)])
        for r in range(4):
            folded[4 * i + r] = fold_rows(acc[r * 8 : r * 8 + 8])
        return 0

    lax.fori_loop(0, 6, outer_planes, 0)
    for k in range(FIELDS):
        sums = jnp.where(iota(1) == k, jnp.sum(folded[k], axis=1, keepdims=True), sums)
    value = (sums + pltpu.roll(pltpu.roll(sums, 4, axis=0), 64, axis=1))[0:4, :]
    pl.semaphore_wait(known.at[1], len(across))
    for s, (dims, plan, slots) in enumerate(zip(STAGES, plans, (slots_one, slots_two))):
        me, size = member(pos, dims), group_size(dims)
        slots[me] = value
        for off in plan:
            pltpu.make_async_remote_copy(
                src_ref=slots.at[me], dst_ref=slots.at[me], send_sem=sum_send.at[s], recv_sem=sum_recv.at[s],
                device_id=device(peer(pos, off)), device_id_type=MESH,
            ).start()
        bulk = slots.at[pl.ds(0, size - 1)]
        pltpu.make_async_copy(bulk, bulk, sum_recv.at[s]).wait()
        value = slots[0]
        for k in range(1, size):
            value = value + slots[k]
    stats[...] = value
    for copy in sends:
        copy.wait_send()
    for s, (dims, slots) in enumerate(zip(STAGES, (slots_one, slots_two))):
        bulk = slots.at[pl.ds(0, group_size(dims) - 1)]
        pltpu.make_async_copy(bulk, bulk, sum_send.at[s]).wait()


def wide(matrix):
    return jnp.concatenate([matrix, jnp.zeros((LANES - matrix.shape[0], LANES), jnp.float32)], axis=0)


def rows_dot(left, right):
    return lax.dot_general(
        left, wide(right), (((1,), (1,)), ((), ())), precision=HIGH, preferred_element_type=jnp.float32
    )


def finish(
    count, fields, stats, out, alpha, beta,
    rest, result, columns, spread, alpha_v, beta_v, store_sem,
):
    row, lane = iota(0), iota(1)
    scaled = stats[...] * (1.0 / count)
    sums = jnp.concatenate([scaled, pltpu.roll(scaled, 64, axis=1)], axis=0)
    first = jnp.where(lane < 16, sums, 0.0)
    norms = jnp.where(lane < 8, pltpu.roll(sums, LANES - 16, axis=1), 0.0)
    metric = [jnp.where(lane < 16, pltpu.roll(sums, LANES - at, axis=1), 0.0) for at in (32, 48)]
    twice = [jnp.where(row + 8 * i == lane, 2.0, 0.0) - metric[i] for i in range(2)]
    metric, twice = (jnp.concatenate(m, axis=0) for m in (metric, twice))
    coeffs = rows_dot(first, twice)
    for k in range(2 * WIDTH):
        spread[k] = jnp.broadcast_to(coeffs[:, k : k + 1], (8, LANES))
    last = jnp.where(lane < 8, pltpu.roll(first, LANES - 8, axis=1), 0.0)
    unit = jnp.where(row == lane, 1.0, 0.0)
    alpha_v[...] = rows_dot(unit, last)[:, 0:WIDTH]
    stores = [pltpu.make_async_copy(alpha_v, alpha, store_sem.at[ORB])]
    stores[0].start()
    gram = norms + rows_dot(rows_dot(coeffs, metric) - first, coeffs) - rows_dot(coeffs, first)
    for j in range(WIDTH):
        columns[j] = jnp.broadcast_to(gram[:, j : j + 1], (8, LANES))

    a = [[jnp.broadcast_to(columns[j, i : i + 1, :], (8, LANES)) for j in range(i + 1)] for i in range(WIDTH)]
    inverse = [[None] * WIDTH for _ in range(WIDTH)]
    upper = jnp.zeros((8, LANES), jnp.float32)
    for j in range(WIDTH):
        inverse[j][j] = lax.rsqrt(a[j][j])
        for i in range(j, WIDTH):
            a[i][j] = a[i][j] * inverse[j][j]
            upper = jnp.where((row == j) & (lane == i), a[i][j], upper)
        for i in range(j + 1, WIDTH):
            for k in range(j + 1, i + 1):
                a[i][k] = a[i][k] - a[i][j] * a[k][j]
    for i in range(WIDTH):
        for j in range(i):
            total = a[i][j] * inverse[j][j]
            for k in range(j + 1, i):
                total = total + a[i][k] * inverse[k][j]
            inverse[i][j] = -(total * inverse[i][i])
    beta_v[...] = upper[:, 0:WIDTH]
    stores.append(pltpu.make_async_copy(beta_v, beta, store_sem.at[ORB + 1]))
    stores[1].start()
    for i in range(WIDTH):
        for j in range(i + 1):
            columns[WIDTH + i * WIDTH + j] = inverse[i][j]

    for orb in range(ORB):

        def residual(m, _):
            for half in range(2):
                tiles = [8 * (4 * half + x) for x in range(4)]
                acc = [[fields[orb, 2 * WIDTH + 2 * m + r, pl.ds(t + 8, 8), :] for t in tiles] for r in range(2)]
                for k in range(2 * WIDTH):
                    c = [jnp.broadcast_to(spread[k, pl.ds(2 * m + r, 1), :], (8, LANES)) for r in range(2)]
                    for x, t in enumerate(tiles):
                        q = fields[orb, k, pl.ds(t + 8, 8), :]
                        for r in range(2):
                            acc[r][x] = acc[r][x] - c[r] * q
                for r in range(2):
                    for x, t in enumerate(tiles):
                        rest[2 * m + r, pl.ds(t, 8), :] = acc[r][x]
            return 0

        lax.fori_loop(0, WIDTH // 2, residual, 0)
        for n in range(WIDTH):
            acc = None
            for m in range(n + 1):
                c = columns[WIDTH + n * WIDTH + m]
                terms = [c * rest[m, 8 * x : 8 * x + 8, :] for x in range(SIDE)]
                acc = terms if acc is None else [p + q for p, q in zip(acc, terms)]
            for x in range(SIDE):
                result[orb, n, 8 * x : 8 * x + 8, :] = acc[x]
        stores.append(pltpu.make_async_copy(result.at[orb], out.at[orb], store_sem.at[orb]))
        stores[-1].start()
    for store in stores:
        store.wait()


def per_device(nx, ny, prev, block, seeds, levels, hop, onsite):
    f32, i32 = jnp.float32, jnp.int32
    shape = block.shape
    prev, block = (v.reshape(ORB, WIDTH, ROWS, LANES) for v in (prev, block))
    hop, onsite = hop.transpose(0, 2, 3, 1), onsite.T
    seeds, levels = seeds.reshape(3, ROWS, LANES), levels.reshape(ROWS, LANES)
    operands = (prev, block, seeds, levels, hop, onsite)
    prev, block, seeds, levels, hop, onsite = (pltpu.with_memory_space_constraint(v, pltpu.HBM) for v in operands)
    hbm, vmem = pl.BlockSpec(memory_space=pltpu.HBM), pl.BlockSpec(memory_space=pltpu.VMEM)
    plane = (2, ORB, WIDTH, 8, LANES)
    dma = pltpu.SemaphoreType.DMA
    every = (ORB, FIELDS, ROWS + 16, LANES)
    values, stats = pl.pallas_call(
        functools.partial(apply_and_reduce, nx, ny),
        out_shape=(jax.ShapeDtypeStruct(every, f32), jax.ShapeDtypeStruct((4, LANES), f32)),
        in_specs=[hbm] * 6,
        out_specs=(vmem, vmem),
        scratch_shapes=[
            pltpu.VMEM((3, ROWS, LANES), i32),
            pltpu.VMEM((ROWS, LANES), i32),
            pltpu.VMEM(hop.shape, f32),
            pltpu.VMEM(onsite.shape, f32),
            pltpu.VMEM((30, 8, LANES), f32),
            pltpu.VMEM((9, ROWS + 8, LANES), f32),
            pltpu.VMEM((9, ROWS, LANES), f32),
            pltpu.VMEM((9, ROWS, LANES), f32),
            pltpu.VMEM((ORB, ROWS, LANES), f32),
            pltpu.VMEM(plane, f32),
            pltpu.VMEM(plane, f32),
            pltpu.VMEM(plane, f32),
            pltpu.VMEM((8, LANES), i32),
            pltpu.VMEM((8, LANES), i32),
            pltpu.VMEM((8, LANES), i32),
            pltpu.VMEM((group_size(STAGES[0]), 4, LANES), f32),
            pltpu.VMEM((group_size(STAGES[1]), 4, LANES), f32),
            pltpu.VMEM((6, 32, 8, LANES), f32),
            pltpu.VMEM((FIELDS, 8, LANES), f32),
            dma((6,)),
            dma((6,)),
            dma((6,)),
            dma((2,)),
            dma((2,)),
            pltpu.SemaphoreType.REGULAR((2,)),
        ],
        compiler_params=pltpu.CompilerParams(
            collective_id=0, has_side_effects=True, vmem_limit_bytes=24 << 20
        ),
    )(prev, block, seeds, levels, hop, onsite)
    count = float(ORB * ROWS * LANES * nx * ny)
    out, alpha, beta = pl.pallas_call(
        functools.partial(finish, count),
        out_shape=(
            jax.ShapeDtypeStruct(block.shape, f32),
            jax.ShapeDtypeStruct((WIDTH, WIDTH), f32),
            jax.ShapeDtypeStruct((WIDTH, WIDTH), f32),
        ),
        in_specs=[vmem, vmem],
        out_specs=(hbm, hbm, hbm),
        scratch_shapes=[
            pltpu.VMEM((WIDTH, ROWS, LANES), f32),
            pltpu.VMEM((ORB, WIDTH, ROWS, LANES), f32),
            pltpu.VMEM((WIDTH + WIDTH * WIDTH, 8, LANES), f32),
            pltpu.VMEM((2 * WIDTH, 8, LANES), f32),
            pltpu.VMEM((WIDTH, WIDTH), f32),
            pltpu.VMEM((WIDTH, WIDTH), f32),
            dma((ORB + 2,)),
        ],
        compiler_params=pltpu.CompilerParams(vmem_limit_bytes=24 << 20),
    )(values, stats)
    return out.reshape(shape), alpha, beta


def solution(mesh):
    fields = P(None, None, "gx", "gy", None)
    return jax.shard_map(
        functools.partial(per_device, mesh.shape["gx"], mesh.shape["gy"]),
        mesh=mesh,
        in_specs=(fields, fields, P(None, "gx", "gy", None), P("gx", "gy", None), P(), P()),
        out_specs=(fields, P(), P()),
        check_vma=False,
    )
```

```python
import functools

import jax
import jax.numpy as jnp
from jax import lax
from jax.experimental import pallas as pl
from jax.experimental.pallas import tpu as pltpu
from jax.sharding import PartitionSpec as P

HIGH = lax.Precision.HIGHEST
MESH = pl.DeviceIdType.MESH
ORB, WIDTH, SIDE, LANES, KINDS = 3, 8, 8, 128, 16
ROWS = SIDE * SIDE
FIELDS = 3 * WIDTH

DIGITS = {"x": 4, "zh": 4, "y": 8, "zl": 2, "core": 2}
STAGES = (("core", "y"), ("x", "zh", "zl"))


def position():
    gx, gy = lax.axis_index("gx"), lax.axis_index("gy")
    return {"x": gx // 4, "zh": gx % 4, "y": gy // 4, "zl": (gy // 2) % 2, "core": gy % 2}


def device(pos):
    return (pos["x"] * 4 + pos["zh"], pos["y"] * 4 + pos["zl"] * 2 + pos["core"])


def group_size(dims):
    size = 1
    for dim in dims:
        size *= DIGITS[dim]
    return size


def member(pos, dims):
    index = 0
    for dim in dims:
        index = index * DIGITS[dim] + pos[dim]
    return index


def offsets(dims):
    found = []
    for k in range(1, group_size(dims)):
        off, rest = {}, k
        for dim in reversed(dims):
            off[dim] = rest % DIGITS[dim]
            rest //= DIGITS[dim]
        hops = 0
        if "y" in off:
            hops += min(off["y"], 8 - off["y"])
        if "x" in off:
            hops += min(off["x"], 4 - off["x"])
        if "zh" in off:
            z = (off["zh"] * 2 + off.get("zl", 0)) % 8
            hops += min(z, 8 - z)
        found.append((-hops, k, off))
    return [off for _, _, off in sorted(found, key=lambda t: t[:2])]


def moved(pos, dim, steps):
    new = dict(pos)
    if dim == "z":
        z = (pos["zh"] * 2 + pos["zl"] + steps) % 8
        new["zh"], new["zl"] = z // 2, z % 2
    else:
        new[dim] = (pos[dim] + steps) % DIGITS[dim]
    return device(new)


def peer(pos, off):
    return {d: (pos[d] + off[d]) % DIGITS[d] if off.get(d) else pos[d] for d in pos}


def iota(axis):
    return lax.broadcasted_iota(jnp.int32, (8, LANES), axis)


def fold_rows(parts):
    row = iota(0)
    for bit in (1, 2, 4):
        low = (row & bit) == 0
        parts = [
            jnp.where(low, a, b) + pltpu.roll(jnp.where(low, b, a), bit, axis=0)
            for a, b in zip(parts[0::2], parts[1::2])
        ]
    return parts[0]


def packed(sums):
    total = sums
    for q in (1, 2, 3):
        total = total + pltpu.roll(pltpu.roll(sums, 8 - 2 * q, axis=0), 32 * q, axis=1)
    return total[0:2, :]


def unpacked(value, spare):
    spare[0:2, :] = value
    for q in (1, 2, 3):
        spare[2 * q : 2 * q + 2, :] = pltpu.roll(value, LANES - 32 * q, axis=1)
    return spare[...]


def products(fields, first, others, planes, acc):
    for x in planes:
        rows = pl.ds(8 * x + 8, 8) if isinstance(x, int) else pl.ds(pl.multiple_of(8 * x + 8, 8), 8)
        for orb in range(ORB):
            left = [fields[orb, first + r, rows, :] for r in range(4)]
            right = [fields[orb, others + s, rows, :] for s in range(8)]
            acc = [acc[r * 8 + s] + left[r] * right[s] for r in range(4) for s in range(8)]
    return acc


def inner_rows(fields, first, others, lane, sums):
    zero = jnp.zeros((8, LANES), jnp.float32)
    acc = lax.fori_loop(0, SIDE, lambda x, acc: tuple(products(fields, first, others, (x,), acc)), (zero,) * 32)
    for r in range(4):
        column = jnp.sum(fold_rows(list(acc[r * 8 : r * 8 + 8])), axis=1, keepdims=True)
        sums = jnp.where(iota(1) == lane + r, column, sums)
    return sums


def picked(table, index):
    return jnp.take_along_axis(table, index, axis=1, mode="promise_in_bounds")


def apply_and_reduce(
    nx, ny, scale, prev, block, seeds, levels, hop, onsite, fields, stats, matrices,
    seed_v, level_v, hop_v, onsite_v, table, coef_x, coef_y, coef_z, energy,
    edge_y, halo_x, halo_y, seed_edge, seed_x, seed_y, slots_one, slots_two, early_one, early_two, partial, folded, spare,
    load_sem, halo_send, halo_recv, sum_send, sum_recv, known,
):
    gx, gy = lax.axis_index("gx"), lax.axis_index("gy")
    right, left = ((gx + 1) % nx, gy), ((gx + nx - 1) % nx, gy)
    above, below = (gx, (gy + 1) % ny), (gx, (gy + ny - 1) % ny)
    pos = position()
    plans = [offsets(dims) for dims in STAGES]

    barrier = pltpu.get_barrier_semaphore()
    rings = [moved(pos, dim, k) for dim in ("z", "y") for k in (1, -1, 2, -2)]
    across = [moved(pos, "x", k) for k in (1, 2, 3)] + [moved(pos, "core", 1)]
    partners = [right, left, above, below] + rings + across

    def greet(sem, devices):
        for other in devices:
            pl.semaphore_signal(sem, inc=1, device_id=other, device_id_type=MESH)

    greet(barrier, partners)

    inside = pl.ds(8, ROWS)
    loads = [
        pltpu.make_async_copy(seeds, seed_v, load_sem.at[0]),
        pltpu.make_async_copy(block, fields.at[:, pl.ds(WIDTH, WIDTH), inside, :], load_sem.at[1]),
        pltpu.make_async_copy(hop, hop_v, load_sem.at[2]),
        pltpu.make_async_copy(onsite, onsite_v, load_sem.at[3]),
        pltpu.make_async_copy(levels, level_v, load_sem.at[4]),
        pltpu.make_async_copy(prev, fields.at[:, pl.ds(0, WIDTH), inside, :], load_sem.at[5]),
    ]
    for load in loads:
        load.start()

    pl.semaphore_wait(barrier, len(partners))
    greet(known.at[0], rings)

    def send(i, src, dst, to):
        return pltpu.make_async_remote_copy(
            src_ref=src, dst_ref=dst, send_sem=halo_send.at[i], recv_sem=halo_recv.at[i],
            device_id=to, device_id_type=MESH,
        )

    last, lead = pl.ds(ROWS - 8, 8), pl.ds(0, 8)
    sends = [
        send(0, seeds.at[0, last, :], seed_x, right),
        send(1, block.at[:, :, last, :], halo_x.at[0], right),
        send(2, block.at[:, :, lead, :], halo_x.at[1], left),
    ]
    for copy in sends:
        copy.start()
    loads[0].wait()
    seed_edge[...] = seed_v[1, pl.ds(7, 8, stride=8), :]
    loads[1].wait()

    def pack(n, _):
        for orb in range(ORB):
            edge_y[0, orb, n] = fields[orb, WIDTH + n, pl.ds(15, 8, stride=8), :]
            edge_y[1, orb, n] = fields[orb, WIDTH + n, pl.ds(8, 8, stride=8), :]
        return 0

    lax.fori_loop(0, WIDTH, pack, 0)
    more = [
        send(3, seed_edge, seed_y, above),
        send(4, edge_y.at[0], halo_y.at[0], above),
        send(5, edge_y.at[1], halo_y.at[1], below),
    ]
    for copy in more:
        copy.start()
    sends += more
    pl.semaphore_wait(known.at[0], len(rings))
    greet(known.at[1], across)

    for load in loads[2:5]:
        load.wait()
    zero = jnp.zeros((8, LANES), jnp.float32)

    for a in range(ORB):
        table[27 + a, :, 0:KINDS] = jnp.broadcast_to(onsite_v[a : a + 1, :], (8, KINDS))
        for d in range(3):
            for b in range(ORB):
                table[d * 9 + a * 3 + b, :, 0:KINDS] = jnp.broadcast_to(hop_v[d, a, b : b + 1, :], (8, KINDS))

    for n in range(WIDTH):
        for orb in range(ORB):
            fields[orb, WIDTH + n, 0:8, :] = zero
            fields[orb, WIDTH + n, ROWS + 8 : ROWS + 16, :] = zero
    for ab in range(9):
        coef_x[ab, 0:8, :] = zero
    inner_row = iota(0) < 7

    def look_up(x, _):
        rows = pl.ds(pl.multiple_of(8 * x, 8), 8)
        later = pl.ds(pl.multiple_of(8 * x + 8, 8), 8)
        at_x, at_y, at_z = (seed_v[d, rows, :] for d in range(3))
        level = level_v[rows, :]
        for a in range(ORB):
            energy[a, rows, :] = picked(table[27 + a], level)
            for b in range(ORB):
                ab = a * 3 + b
                coef_x[ab, later, :] = picked(table[ab], at_x)
                coef_y[ab, rows, :] = jnp.where(inner_row, picked(table[9 + ab], at_y), 0.0)
                coef_z[ab, rows, :] = picked(table[18 + ab], at_z)
        return 0

    lax.fori_loop(0, SIDE, look_up, 0)

    def own(x, _):
        before = pl.ds(pl.multiple_of(8 * x, 8), 8)
        here = pl.ds(pl.multiple_of(8 * x + 8, 8), 8)
        after = pl.ds(pl.multiple_of(8 * x + 16, 8), 8)
        cx = [coef_x[ab, here, :] for ab in range(9)]
        cm = [coef_x[ab, before, :] for ab in range(9)]
        cy = [coef_y[ab, before, :] for ab in range(9)]
        cz = [coef_z[ab, before, :] for ab in range(9)]
        ce = [energy[a, before, :] for a in range(ORB)]
        for n in range(WIDTH):
            v = [fields[b, WIDTH + n, here, :] for b in range(ORB)]
            vp = [fields[b, WIDTH + n, after, :] for b in range(ORB)]
            vm = [fields[b, WIDTH + n, before, :] for b in range(ORB)]
            vz = [pltpu.roll(u, LANES - 1, axis=1) for u in v]
            vy = [pltpu.roll(u, 7, axis=0) for u in v]
            for a in range(ORB):
                carried_z = cz[a] * v[0] + cz[3 + a] * v[1] + cz[6 + a] * v[2]
                carried_y = cy[a] * v[0] + cy[3 + a] * v[1] + cy[6 + a] * v[2]
                out = ce[a] * v[a] + pltpu.roll(carried_z, 1, axis=1) + pltpu.roll(carried_y, 1, axis=0)
                for b in range(ORB):
                    out = out + cx[a * 3 + b] * vp[b] + cm[b * 3 + a] * vm[b]
                    out = out + cz[a * 3 + b] * vz[b] + cy[a * 3 + b] * vy[b]
                fields[a, 2 * WIDTH + n, here, :] = out
        return 0

    lax.fori_loop(0, SIDE, own, 0)

    def share(stage, slots, sem, value):
        me = member(pos, STAGES[stage])
        slots[me] = value
        for off in plans[stage]:
            pltpu.make_async_remote_copy(
                src_ref=slots.at[me], dst_ref=slots.at[me], send_sem=sum_send.at[sem], recv_sem=sum_recv.at[sem],
                device_id=device(peer(pos, off)), device_id_type=MESH,
            ).start()

    def bulk_wait(stage, slots, sems):
        bulk = slots.at[pl.ds(0, group_size(STAGES[stage]) - 1)]
        pltpu.make_async_copy(bulk, bulk, sems).wait()

    def gathered(stage, slots, sem):
        bulk_wait(stage, slots, sum_recv.at[sem])
        value = slots[0]
        for k in range(1, group_size(STAGES[stage])):
            value = value + slots[k]
        return value

    loads[5].wait()

    def basis_rows(i, sums):
        sums = inner_rows(fields, 4 * i, 0, 4 * i, sums)
        return inner_rows(fields, 4 * i, WIDTH, 16 + 4 * i, sums)

    sums = lax.fori_loop(0, 4, basis_rows, zero)
    early = packed(sums)

    for i in (3, 4, 5):
        sends[i].wait_recv()
    cb = [picked(table[9 + ab], seed_y[...]) for ab in range(9)]
    cf = [picked(table[9 + ab], seed_edge[...]) for ab in range(9)]

    def edges_y(n, _):
        for a in range(ORB):
            field = fields.at[a, 2 * WIDTH + n]
            low, high = field[pl.ds(8, 8, stride=8), :], field[pl.ds(15, 8, stride=8), :]
            for b in range(ORB):
                low = low + cb[b * 3 + a] * halo_y[0, b, n]
                high = high + cf[a * 3 + b] * halo_y[1, b, n]
            field[pl.ds(8, 8, stride=8), :] = low
            field[pl.ds(15, 8, stride=8), :] = high
        return 0

    lax.fori_loop(0, WIDTH, edges_y, 0)

    def inner_planes(i, _):
        acc = lax.fori_loop(
            1, SIDE - 1, lambda x, acc: tuple(products(fields, 4 * i, 2 * WIDTH, (x,), acc)), (zero,) * 32
        )
        for k in range(32):
            partial[i, k] = acc[k]
        return 0

    lax.fori_loop(0, 6, inner_planes, 0)
    pl.semaphore_wait(known.at[1], len(across))
    share(0, early_one, 2, early)

    for i in (0, 1, 2):
        sends[i].wait_recv()
    cm = [picked(table[ab], seed_x[...]) for ab in range(9)]
    cp = [coef_x[ab, ROWS : ROWS + 8, :] for ab in range(9)]

    def edges_x(n, _):
        for a in range(ORB):
            field = fields.at[a, 2 * WIDTH + n]
            low, high = field[8:16, :], field[ROWS : ROWS + 8, :]
            for b in range(ORB):
                low = low + cm[b * 3 + a] * halo_x[0, b, n]
                high = high + cp[a * 3 + b] * halo_x[1, b, n]
            field[8:16, :] = low
            field[ROWS : ROWS + 8, :] = high
        return 0

    lax.fori_loop(0, WIDTH, edges_x, 0)

    def outer_planes(i, _):
        acc = products(fields, 4 * i, 2 * WIDTH, (0, SIDE - 1), [partial[i, k] for k in range(32)])
        for r in range(4):
            folded[4 * i + r] = fold_rows(acc[r * 8 : r * 8 + 8])
        return 0

    lax.fori_loop(0, 6, outer_planes, 0)
    sums = zero
    for k in range(FIELDS):
        sums = jnp.where(iota(1) == k, jnp.sum(folded[k], axis=1, keepdims=True), sums)
    share(0, slots_one, 0, packed(sums))
    share(1, early_two, 3, gathered(0, early_one, 2))

    share(1, slots_two, 1, gathered(0, slots_one, 0))

    both = unpacked(gathered(1, early_two, 3), spare) * scale
    row, lane = iota(0), iota(1)
    metric = [jnp.where(lane < 16, both, 0.0), jnp.where(lane < 16, pltpu.roll(both, LANES - 16, axis=1), 0.0)]
    twice = [jnp.where(row + 8 * i == lane, 2.0, 0.0) - metric[i] for i in range(2)]
    metric, twice = (jnp.concatenate(m, axis=0) for m in (metric, twice))
    matrices[0] = twice
    matrices[1] = 2.0 * twice - rows_dot(rows_dot(twice, metric), twice)

    stats[...] = unpacked(gathered(1, slots_two, 1), spare) * scale
    for copy in sends:
        copy.wait_send()
    for sem, slots in enumerate((slots_one, slots_two, early_one, early_two)):
        bulk_wait(sem % 2, slots, sum_send.at[sem])


def wide(matrix):
    return jnp.concatenate([matrix, jnp.zeros((LANES - matrix.shape[0], LANES), jnp.float32)], axis=0)


def rows_dot(left, right):
    return lax.dot_general(
        left, wide(right), (((1,), (1,)), ((), ())), precision=HIGH, preferred_element_type=jnp.float32
    )


def finish(
    fields, stats, matrices, out, alpha, beta,
    rest, result, columns, spread, alpha_v, beta_v, store_sem,
):
    row, lane = iota(0), iota(1)
    first = jnp.where(lane < 16, stats[...], 0.0)
    norms = jnp.where(lane < 8, pltpu.roll(stats[...], LANES - 16, axis=1), 0.0)
    coeffs = rows_dot(first, matrices[0])
    for k in range(2 * WIDTH):
        spread[k] = jnp.broadcast_to(coeffs[:, k : k + 1], (8, LANES))
    last = jnp.where(lane < 8, pltpu.roll(first, LANES - 8, axis=1), 0.0)
    unit = jnp.where(row == lane, 1.0, 0.0)
    alpha_v[...] = rows_dot(unit, last)[:, 0:WIDTH]
    stores = [pltpu.make_async_copy(alpha_v, alpha, store_sem.at[ORB])]
    stores[0].start()
    gram = norms - rows_dot(rows_dot(first, matrices[1]), first)
    for j in range(WIDTH):
        columns[j] = jnp.broadcast_to(gram[:, j : j + 1], (8, LANES))

    a = [[jnp.broadcast_to(columns[j, i : i + 1, :], (8, LANES)) for j in range(i + 1)] for i in range(WIDTH)]
    inverse = [[None] * WIDTH for _ in range(WIDTH)]
    upper = jnp.zeros((8, LANES), jnp.float32)
    for j in range(WIDTH):
        inverse[j][j] = lax.rsqrt(a[j][j])
        for i in range(j, WIDTH):
            a[i][j] = a[i][j] * inverse[j][j]
            upper = jnp.where((row == j) & (lane == i), a[i][j], upper)
        for i in range(j + 1, WIDTH):
            for k in range(j + 1, i + 1):
                a[i][k] = a[i][k] - a[i][j] * a[k][j]
    for i in range(WIDTH):
        for j in range(i):
            total = a[i][j] * inverse[j][j]
            for k in range(j + 1, i):
                total = total + a[i][k] * inverse[k][j]
            inverse[i][j] = -(total * inverse[i][i])
    beta_v[...] = upper[:, 0:WIDTH]
    stores.append(pltpu.make_async_copy(beta_v, beta, store_sem.at[ORB + 1]))
    stores[1].start()
    for i in range(WIDTH):
        for j in range(i + 1):
            columns[WIDTH + i * WIDTH + j] = inverse[i][j]

    for orb in range(ORB):

        def residual(m, _):
            for half in range(2):
                tiles = [8 * (4 * half + x) for x in range(4)]
                acc = [[fields[orb, 2 * WIDTH + 2 * m + r, pl.ds(t + 8, 8), :] for t in tiles] for r in range(2)]
                for k in range(2 * WIDTH):
                    c = [jnp.broadcast_to(spread[k, pl.ds(2 * m + r, 1), :], (8, LANES)) for r in range(2)]
                    for x, t in enumerate(tiles):
                        q = fields[orb, k, pl.ds(t + 8, 8), :]
                        for r in range(2):
                            acc[r][x] = acc[r][x] - c[r] * q
                for r in range(2):
                    for x, t in enumerate(tiles):
                        rest[2 * m + r, pl.ds(t, 8), :] = acc[r][x]
            return 0

        lax.fori_loop(0, WIDTH // 2, residual, 0)
        for n in range(WIDTH):
            acc = None
            for m in range(n + 1):
                c = columns[WIDTH + n * WIDTH + m]
                terms = [c * rest[m, 8 * x : 8 * x + 8, :] for x in range(SIDE)]
                acc = terms if acc is None else [p + q for p, q in zip(acc, terms)]
            for x in range(SIDE):
                result[orb, n, 8 * x : 8 * x + 8, :] = acc[x]
        stores.append(pltpu.make_async_copy(result.at[orb], out.at[orb], store_sem.at[orb]))
        stores[-1].start()
    for store in stores:
        store.wait()


def per_device(nx, ny, prev, block, seeds, levels, hop, onsite):
    f32, i32 = jnp.float32, jnp.int32
    shape = block.shape
    prev, block = (v.reshape(ORB, WIDTH, ROWS, LANES) for v in (prev, block))
    hop, onsite = hop.transpose(0, 2, 3, 1), onsite.T
    seeds, levels = seeds.reshape(3, ROWS, LANES), levels.reshape(ROWS, LANES)
    operands = (prev, block, seeds, levels, hop, onsite)
    prev, block, seeds, levels, hop, onsite = (pltpu.with_memory_space_constraint(v, pltpu.HBM) for v in operands)
    hbm, vmem = pl.BlockSpec(memory_space=pltpu.HBM), pl.BlockSpec(memory_space=pltpu.VMEM)
    plane = (2, ORB, WIDTH, 8, LANES)
    dma = pltpu.SemaphoreType.DMA
    every = (ORB, FIELDS, ROWS + 16, LANES)
    values, stats, matrices = pl.pallas_call(
        functools.partial(apply_and_reduce, nx, ny, 1.0 / (ORB * ROWS * LANES * nx * ny)),
        out_shape=tuple(jax.ShapeDtypeStruct(v, f32) for v in (every, (8, LANES), (2, 2 * WIDTH, LANES))),
        in_specs=[hbm] * 6,
        out_specs=(vmem, vmem, vmem),
        scratch_shapes=[
            pltpu.VMEM((3, ROWS, LANES), i32),
            pltpu.VMEM((ROWS, LANES), i32),
            pltpu.VMEM(hop.shape, f32),
            pltpu.VMEM(onsite.shape, f32),
            pltpu.VMEM((30, 8, LANES), f32),
            pltpu.VMEM((9, ROWS + 8, LANES), f32),
            pltpu.VMEM((9, ROWS, LANES), f32),
            pltpu.VMEM((9, ROWS, LANES), f32),
            pltpu.VMEM((ORB, ROWS, LANES), f32),
            pltpu.VMEM(plane, f32),
            pltpu.VMEM(plane, f32),
            pltpu.VMEM(plane, f32),
            pltpu.VMEM((8, LANES), i32),
            pltpu.VMEM((8, LANES), i32),
            pltpu.VMEM((8, LANES), i32),
            pltpu.VMEM((group_size(STAGES[0]), 2, LANES), f32),
            pltpu.VMEM((group_size(STAGES[1]), 2, LANES), f32),
            pltpu.VMEM((group_size(STAGES[0]), 2, LANES), f32),
            pltpu.VMEM((group_size(STAGES[1]), 2, LANES), f32),
            pltpu.VMEM((6, 32, 8, LANES), f32),
            pltpu.VMEM((FIELDS, 8, LANES), f32),
            pltpu.VMEM((8, LANES), f32),
            dma((6,)),
            dma((6,)),
            dma((6,)),
            dma((4,)),
            dma((4,)),
            pltpu.SemaphoreType.REGULAR((2,)),
        ],
        compiler_params=pltpu.CompilerParams(
            collective_id=0, has_side_effects=True, vmem_limit_bytes=24 << 20
        ),
    )(prev, block, seeds, levels, hop, onsite)
    out, alpha, beta = pl.pallas_call(
        finish,
        out_shape=(
            jax.ShapeDtypeStruct(block.shape, f32),
            jax.ShapeDtypeStruct((WIDTH, WIDTH), f32),
            jax.ShapeDtypeStruct((WIDTH, WIDTH), f32),
        ),
        in_specs=[vmem, vmem, vmem],
        out_specs=(hbm, hbm, hbm),
        scratch_shapes=[
            pltpu.VMEM((WIDTH, ROWS, LANES), f32),
            pltpu.VMEM((ORB, WIDTH, ROWS, LANES), f32),
            pltpu.VMEM((WIDTH + WIDTH * WIDTH, 8, LANES), f32),
            pltpu.VMEM((2 * WIDTH, 8, LANES), f32),
            pltpu.VMEM((WIDTH, WIDTH), f32),
            pltpu.VMEM((WIDTH, WIDTH), f32),
            dma((ORB + 2,)),
        ],
        compiler_params=pltpu.CompilerParams(vmem_limit_bytes=24 << 20),
    )(values, stats, matrices)
    return out.reshape(shape), alpha, beta


def solution(mesh):
    fields = P(None, None, "gx", "gy", None)
    return jax.shard_map(
        functools.partial(per_device, mesh.shape["gx"], mesh.shape["gy"]),
        mesh=mesh,
        in_specs=(fields, fields, P(None, "gx", "gy", None), P("gx", "gy", None), P(), P()),
        out_specs=(fields, P(), P()),
        check_vma=False,
    )
```

```python
import functools

import jax
import jax.numpy as jnp
from jax import lax
from jax.experimental import pallas as pl
from jax.experimental.pallas import tpu as pltpu
from jax.sharding import PartitionSpec as P

HIGH = lax.Precision.HIGHEST
MESH = pl.DeviceIdType.MESH
ORB, WIDTH, SIDE, LANES, KINDS = 3, 8, 8, 128, 16
ROWS = SIDE * SIDE
PART = 32
FIELDS = 3 * WIDTH

DIGITS = {"x": 4, "zh": 4, "y": 8, "zl": 2, "core": 2}
STAGES = (("core", "y"), ("x", "zh", "zl"))


def position():
    gx, gy = lax.axis_index("gx"), lax.axis_index("gy")
    return {"x": gx // 4, "zh": gx % 4, "y": gy // 4, "zl": (gy // 2) % 2, "core": gy % 2}


def device(pos):
    return (pos["x"] * 4 + pos["zh"], pos["y"] * 4 + pos["zl"] * 2 + pos["core"])


def group_size(dims):
    size = 1
    for dim in dims:
        size *= DIGITS[dim]
    return size


def member(pos, dims):
    index = 0
    for dim in dims:
        index = index * DIGITS[dim] + pos[dim]
    return index


def offsets(dims):
    found = []
    for k in range(1, group_size(dims)):
        off, rest = {}, k
        for dim in reversed(dims):
            off[dim] = rest % DIGITS[dim]
            rest //= DIGITS[dim]
        hops = 0
        if "y" in off:
            hops += min(off["y"], 8 - off["y"])
        if "x" in off:
            hops += min(off["x"], 4 - off["x"])
        if "zh" in off:
            z = (off["zh"] * 2 + off.get("zl", 0)) % 8
            hops += min(z, 8 - z)
        found.append((-hops, k, off))
    return [off for _, _, off in sorted(found, key=lambda t: t[:2])]


def moved(pos, dim, steps):
    new = dict(pos)
    if dim == "z":
        z = (pos["zh"] * 2 + pos["zl"] + steps) % 8
        new["zh"], new["zl"] = z // 2, z % 2
    else:
        new[dim] = (pos[dim] + steps) % DIGITS[dim]
    return device(new)


def peer(pos, off):
    return {d: (pos[d] + off[d]) % DIGITS[d] if off.get(d) else pos[d] for d in pos}


def iota(axis):
    return lax.broadcasted_iota(jnp.int32, (8, LANES), axis)


def fold_rows(parts):
    row = iota(0)
    for bit in (1, 2, 4):
        low = (row & bit) == 0
        parts = [
            jnp.where(low, a, b) + pltpu.roll(jnp.where(low, b, a), bit, axis=0)
            for a, b in zip(parts[0::2], parts[1::2])
        ]
    return parts[0]


def packed(sums):
    total = sums
    for q in (1, 2, 3):
        total = total + pltpu.roll(pltpu.roll(sums, 8 - 2 * q, axis=0), 32 * q, axis=1)
    return total[0:2, :]


def unpacked(value, spare):
    spare[0:2, :] = value
    for q in (1, 2, 3):
        spare[2 * q : 2 * q + 2, :] = pltpu.roll(value, LANES - 32 * q, axis=1)
    return spare[...]


def products(fields, first, others, planes, acc):
    for x in planes:
        rows = pl.ds(8 * x + 8, 8) if isinstance(x, int) else pl.ds(pl.multiple_of(8 * x + 8, 8), 8)
        for orb in range(ORB):
            left = [fields[orb, first + r, rows, :] for r in range(4)]
            right = [fields[orb, others + s, rows, :] for s in range(8)]
            acc = [acc[r * 8 + s] + left[r] * right[s] for r in range(4) for s in range(8)]
    return acc


def inner_rows(fields, first, others, lane, sums):
    zero = jnp.zeros((8, LANES), jnp.float32)
    acc = lax.fori_loop(0, SIDE, lambda x, acc: tuple(products(fields, first, others, (x,), acc)), (zero,) * 32)
    for r in range(4):
        column = jnp.sum(fold_rows(list(acc[r * 8 : r * 8 + 8])), axis=1, keepdims=True)
        sums = jnp.where(iota(1) == lane + r, column, sums)
    return sums


def terms(value):
    found = []
    for _ in range(3):
        term = value.astype(jnp.bfloat16)
        found.append(term)
        value = value - term.astype(jnp.float32)
    return found


def picked(table, index):
    return jnp.take_along_axis(table, index, axis=1, mode="promise_in_bounds")


def apply_and_reduce(
    nx, ny, scale, prev, block, seeds, levels, hop, onsite, stats, matrices, lines,
    fields, seed_v, level_v, hop_v, onsite_v, table, coef_x, coef_y, coef_z, energy,
    edge_y, halo_x, halo_y, seed_edge, seed_x, seed_y, slots_one, slots_two, early_one, early_two, partial, folded, spare,
    load_sem, halo_send, halo_recv, sum_send, sum_recv, known,
):
    gx, gy = lax.axis_index("gx"), lax.axis_index("gy")
    right, left = ((gx + 1) % nx, gy), ((gx + nx - 1) % nx, gy)
    above, below = (gx, (gy + 1) % ny), (gx, (gy + ny - 1) % ny)
    pos = position()
    plans = [offsets(dims) for dims in STAGES]

    barrier = pltpu.get_barrier_semaphore()
    rings = [moved(pos, dim, k) for dim in ("z", "y") for k in (1, -1, 2, -2)]
    across = [moved(pos, "x", k) for k in (1, 2, 3)] + [moved(pos, "core", 1)]
    partners = [right, left, above, below] + rings + across

    def greet(sem, devices):
        for other in devices:
            pl.semaphore_signal(sem, inc=1, device_id=other, device_id_type=MESH)

    greet(barrier, partners)

    inside = pl.ds(8, ROWS)
    loads = [
        pltpu.make_async_copy(seeds, seed_v, load_sem.at[0]),
        pltpu.make_async_copy(block, fields.at[:, pl.ds(WIDTH, WIDTH), inside, :], load_sem.at[1]),
        pltpu.make_async_copy(hop, hop_v, load_sem.at[2]),
        pltpu.make_async_copy(onsite, onsite_v, load_sem.at[3]),
        pltpu.make_async_copy(levels, level_v, load_sem.at[4]),
        pltpu.make_async_copy(prev, fields.at[:, pl.ds(0, WIDTH), inside, :], load_sem.at[5]),
    ]
    for load in loads:
        load.start()

    pl.semaphore_wait(barrier, len(partners))
    greet(known.at[0], rings)

    def send(i, src, dst, to):
        return pltpu.make_async_remote_copy(
            src_ref=src, dst_ref=dst, send_sem=halo_send.at[i], recv_sem=halo_recv.at[i],
            device_id=to, device_id_type=MESH,
        )

    last, lead = pl.ds(ROWS - 8, 8), pl.ds(0, 8)
    sends = [
        send(0, seeds.at[0, last, :], seed_x, right),
        send(1, block.at[:, :, last, :], halo_x.at[0], right),
        send(2, block.at[:, :, lead, :], halo_x.at[1], left),
    ]
    for copy in sends:
        copy.start()
    loads[0].wait()
    seed_edge[...] = seed_v[1, pl.ds(7, 8, stride=8), :]
    loads[1].wait()

    def pack(n, _):
        for orb in range(ORB):
            edge_y[0, orb, n] = fields[orb, WIDTH + n, pl.ds(15, 8, stride=8), :]
            edge_y[1, orb, n] = fields[orb, WIDTH + n, pl.ds(8, 8, stride=8), :]
        return 0

    lax.fori_loop(0, WIDTH, pack, 0)
    more = [
        send(3, seed_edge, seed_y, above),
        send(4, edge_y.at[0], halo_y.at[0], above),
        send(5, edge_y.at[1], halo_y.at[1], below),
    ]
    for copy in more:
        copy.start()
    sends += more
    pl.semaphore_wait(known.at[0], len(rings))
    greet(known.at[1], across)

    for load in loads[2:5]:
        load.wait()
    zero = jnp.zeros((8, LANES), jnp.float32)

    for a in range(ORB):
        table[27 + a, :, 0:KINDS] = jnp.broadcast_to(onsite_v[a : a + 1, :], (8, KINDS))
        for d in range(3):
            for b in range(ORB):
                table[d * 9 + a * 3 + b, :, 0:KINDS] = jnp.broadcast_to(hop_v[d, a, b : b + 1, :], (8, KINDS))

    for n in range(WIDTH):
        for orb in range(ORB):
            fields[orb, WIDTH + n, 0:8, :] = zero
            fields[orb, WIDTH + n, ROWS + 8 : ROWS + 16, :] = zero
    for ab in range(9):
        coef_x[ab, 0:8, :] = zero
    inner_row = iota(0) < 7

    def look_up(x, _):
        rows = pl.ds(pl.multiple_of(8 * x, 8), 8)
        later = pl.ds(pl.multiple_of(8 * x + 8, 8), 8)
        at_x, at_y, at_z = (seed_v[d, rows, :] for d in range(3))
        level = level_v[rows, :]
        for a in range(ORB):
            energy[a, rows, :] = picked(table[27 + a], level)
            for b in range(ORB):
                ab = a * 3 + b
                coef_x[ab, later, :] = picked(table[ab], at_x)
                coef_y[ab, rows, :] = jnp.where(inner_row, picked(table[9 + ab], at_y), 0.0)
                coef_z[ab, rows, :] = picked(table[18 + ab], at_z)
        return 0

    lax.fori_loop(0, SIDE, look_up, 0)

    def own(x, _):
        before = pl.ds(pl.multiple_of(8 * x, 8), 8)
        here = pl.ds(pl.multiple_of(8 * x + 8, 8), 8)
        after = pl.ds(pl.multiple_of(8 * x + 16, 8), 8)
        cx = [coef_x[ab, here, :] for ab in range(9)]
        cm = [coef_x[ab, before, :] for ab in range(9)]
        cy = [coef_y[ab, before, :] for ab in range(9)]
        cz = [coef_z[ab, before, :] for ab in range(9)]
        ce = [energy[a, before, :] for a in range(ORB)]
        for n in range(WIDTH):
            v = [fields[b, WIDTH + n, here, :] for b in range(ORB)]
            vp = [fields[b, WIDTH + n, after, :] for b in range(ORB)]
            vm = [fields[b, WIDTH + n, before, :] for b in range(ORB)]
            vz = [pltpu.roll(u, LANES - 1, axis=1) for u in v]
            vy = [pltpu.roll(u, 7, axis=0) for u in v]
            for a in range(ORB):
                carried_z = cz[a] * v[0] + cz[3 + a] * v[1] + cz[6 + a] * v[2]
                carried_y = cy[a] * v[0] + cy[3 + a] * v[1] + cy[6 + a] * v[2]
                out = ce[a] * v[a] + pltpu.roll(carried_z, 1, axis=1) + pltpu.roll(carried_y, 1, axis=0)
                for b in range(ORB):
                    out = out + cx[a * 3 + b] * vp[b] + cm[b * 3 + a] * vm[b]
                    out = out + cz[a * 3 + b] * vz[b] + cy[a * 3 + b] * vy[b]
                fields[a, 2 * WIDTH + n, here, :] = out
        return 0

    lax.fori_loop(0, SIDE, own, 0)

    def share(stage, slots, sem, value):
        me = member(pos, STAGES[stage])
        slots[me] = value
        for off in plans[stage]:
            pltpu.make_async_remote_copy(
                src_ref=slots.at[me], dst_ref=slots.at[me], send_sem=sum_send.at[sem], recv_sem=sum_recv.at[sem],
                device_id=device(peer(pos, off)), device_id_type=MESH,
            ).start()

    def bulk_wait(stage, slots, sems):
        bulk = slots.at[pl.ds(0, group_size(STAGES[stage]) - 1)]
        pltpu.make_async_copy(bulk, bulk, sems).wait()

    def gathered(stage, slots, sem):
        bulk_wait(stage, slots, sum_recv.at[sem])
        value = slots[0]
        for k in range(1, group_size(STAGES[stage])):
            value = value + slots[k]
        return value

    loads[5].wait()

    def basis_rows(i, sums):
        sums = inner_rows(fields, 4 * i, 0, 4 * i, sums)
        return inner_rows(fields, 4 * i, WIDTH, 16 + 4 * i, sums)

    sums = lax.fori_loop(0, 4, basis_rows, zero)
    early = packed(sums)

    for i in (3, 4, 5):
        sends[i].wait_recv()
    cb = [picked(table[9 + ab], seed_y[...]) for ab in range(9)]
    cf = [picked(table[9 + ab], seed_edge[...]) for ab in range(9)]

    def edges_y(n, _):
        for a in range(ORB):
            field = fields.at[a, 2 * WIDTH + n]
            low, high = field[pl.ds(8, 8, stride=8), :], field[pl.ds(15, 8, stride=8), :]
            for b in range(ORB):
                low = low + cb[b * 3 + a] * halo_y[0, b, n]
                high = high + cf[a * 3 + b] * halo_y[1, b, n]
            field[pl.ds(8, 8, stride=8), :] = low
            field[pl.ds(15, 8, stride=8), :] = high
        return 0

    lax.fori_loop(0, WIDTH, edges_y, 0)

    def inner_planes(i, _):
        acc = lax.fori_loop(
            1, SIDE - 1, lambda x, acc: tuple(products(fields, 4 * i, 2 * WIDTH, (x,), acc)), (zero,) * 32
        )
        for k in range(32):
            partial[i, k] = acc[k]
        return 0

    lax.fori_loop(0, 6, inner_planes, 0)
    pl.semaphore_wait(known.at[1], len(across))
    share(0, early_one, 2, early)

    for i in (0, 1, 2):
        sends[i].wait_recv()
    cm = [picked(table[ab], seed_x[...]) for ab in range(9)]
    cp = [coef_x[ab, ROWS : ROWS + 8, :] for ab in range(9)]

    def edges_x(n, _):
        for a in range(ORB):
            field = fields.at[a, 2 * WIDTH + n]
            low, high = field[8:16, :], field[ROWS : ROWS + 8, :]
            for b in range(ORB):
                low = low + cm[b * 3 + a] * halo_x[0, b, n]
                high = high + cp[a * 3 + b] * halo_x[1, b, n]
            field[8:16, :] = low
            field[ROWS : ROWS + 8, :] = high
        return 0

    lax.fori_loop(0, WIDTH, edges_x, 0)

    def outer_planes(i, _):
        acc = products(fields, 4 * i, 2 * WIDTH, (0, SIDE - 1), [partial[i, k] for k in range(32)])
        for r in range(4):
            folded[4 * i + r] = fold_rows(acc[r * 8 : r * 8 + 8])
        return 0

    lax.fori_loop(0, 6, outer_planes, 0)
    sums = zero
    for k in range(FIELDS):
        sums = jnp.where(iota(1) == k, jnp.sum(folded[k], axis=1, keepdims=True), sums)
    share(0, slots_one, 0, packed(sums))

    flat = fields.reshape(ORB, FIELDS * (ROWS + 16), LANES)
    padding = jnp.zeros((PART - FIELDS, LANES), jnp.float32)

    def line_terms(orb):
        def step(x, _):
            for y in range(8):
                value = flat[orb, pl.ds(8 * x + 8 + y, FIELDS, stride=ROWS + 16), :]
                value = jnp.concatenate([value, padding], axis=0)
                for i, term in enumerate(terms(value)):
                    lines[orb, 8 * x + y, i * PART : (i + 1) * PART, :] = term
            return 0

        lax.fori_loop(0, SIDE, step, 0)

    line_terms(0)
    share(1, early_two, 3, gathered(0, early_one, 2))

    share(1, slots_two, 1, gathered(0, slots_one, 0))
    line_terms(1)
    line_terms(2)

    both = unpacked(gathered(1, early_two, 3), spare) * scale
    row, lane = iota(0), iota(1)
    metric = [jnp.where(lane < 16, both, 0.0), jnp.where(lane < 16, pltpu.roll(both, LANES - 16, axis=1), 0.0)]
    twice = [jnp.where(row + 8 * i == lane, 2.0, 0.0) - metric[i] for i in range(2)]
    metric, twice = (jnp.concatenate(m, axis=0) for m in (metric, twice))
    matrices[0] = twice
    matrices[1] = 2.0 * twice - rows_dot(rows_dot(twice, metric), twice)

    stats[...] = unpacked(gathered(1, slots_two, 1), spare) * scale
    for copy in sends:
        copy.wait_send()
    for sem, slots in enumerate((slots_one, slots_two, early_one, early_two)):
        bulk_wait(sem % 2, slots, sum_send.at[sem])


def wide(matrix):
    return jnp.concatenate([matrix, jnp.zeros((LANES - matrix.shape[0], LANES), jnp.float32)], axis=0)


def rows_dot(left, right):
    return lax.dot_general(
        left, wide(right), (((1,), (1,)), ((), ())), precision=HIGH, preferred_element_type=jnp.float32
    )


def finish(
    lines, stats, matrices, out, alpha, beta,
    result, columns, alpha_v, beta_v, store_sem,
):
    row, lane = iota(0), iota(1)
    first = jnp.where(lane < 16, stats[...], 0.0)
    norms = jnp.where(lane < 8, pltpu.roll(stats[...], LANES - 16, axis=1), 0.0)
    coeffs = rows_dot(first, matrices[0])
    last = jnp.where(lane < 8, pltpu.roll(first, LANES - 8, axis=1), 0.0)
    unit = jnp.where(row == lane, 1.0, 0.0)
    alpha_v[...] = rows_dot(unit, last)[:, 0:WIDTH]
    stores = [pltpu.make_async_copy(alpha_v, alpha, store_sem.at[ORB])]
    stores[0].start()
    gram = norms - rows_dot(rows_dot(first, matrices[1]), first)
    for j in range(WIDTH):
        columns[j] = jnp.broadcast_to(gram[:, j : j + 1], (8, LANES))

    a = [[jnp.broadcast_to(columns[j, i : i + 1, :], (8, LANES)) for j in range(i + 1)] for i in range(WIDTH)]
    inverse = [[None] * WIDTH for _ in range(WIDTH)]
    upper = jnp.zeros((8, LANES), jnp.float32)
    for j in range(WIDTH):
        inverse[j][j] = lax.rsqrt(a[j][j])
        for i in range(j, WIDTH):
            a[i][j] = a[i][j] * inverse[j][j]
            upper = jnp.where((row == j) & (lane == i), a[i][j], upper)
        for i in range(j + 1, WIDTH):
            for k in range(j + 1, i + 1):
                a[i][k] = a[i][k] - a[i][j] * a[k][j]
    for i in range(WIDTH):
        for j in range(i):
            total = a[i][j] * inverse[j][j]
            for k in range(j + 1, i):
                total = total + a[i][k] * inverse[k][j]
            inverse[i][j] = -(total * inverse[i][i])
    beta_v[...] = upper[:, 0:WIDTH]
    stores.append(pltpu.make_async_copy(beta_v, beta, store_sem.at[ORB + 1]))
    stores[1].start()
    weights = jnp.zeros((8, LANES), jnp.float32)
    for m in range(WIDTH):
        column = jnp.zeros((8, LANES), jnp.float32)
        for n in range(m, WIDTH):
            column = jnp.where(row == n, inverse[n][m], column)
        weights = weights - column * jnp.broadcast_to(coeffs[m : m + 1, :], (8, LANES))
        weights = jnp.where(lane == 2 * WIDTH + m, column, weights)
    high, middle, low = (term.astype(jnp.float32) for term in terms(weights))
    shifted = [[pltpu.roll(t, PART * i, axis=1) if i else t for i in range(c)] for t, c in ((high, 3), (middle, 2), (low, 1))]
    matrix = jnp.concatenate([sum(group[1:], group[0]) for group in shifted], axis=0).astype(jnp.bfloat16)
    matrix = matrix[:, : 3 * PART]

    for orb in range(ORB):

        for x in range(SIDE):
            for y in range(0, 8, 2):
                pair = jnp.concatenate([lines[orb, 8 * x + y + i] for i in range(2)], axis=1)
                got = jnp.dot(matrix, pair, preferred_element_type=jnp.float32)
                got = got[0:8] + got[8:16] + got[16:24]
                for i in range(2):
                    result[orb, pl.ds(8 * x + y + i, 8, stride=ROWS), :] = got[:, i * LANES : (i + 1) * LANES]
        stores.append(pltpu.make_async_copy(result.at[orb], out.at[orb], store_sem.at[orb]))
        stores[-1].start()
    for store in stores:
        store.wait()


def per_device(nx, ny, prev, block, seeds, levels, hop, onsite):
    f32, i32 = jnp.float32, jnp.int32
    shape = block.shape
    prev, block = (v.reshape(ORB, WIDTH, ROWS, LANES) for v in (prev, block))
    hop, onsite = hop.transpose(0, 2, 3, 1), onsite.T
    seeds, levels = seeds.reshape(3, ROWS, LANES), levels.reshape(ROWS, LANES)
    operands = (prev, block, seeds, levels, hop, onsite)
    prev, block, seeds, levels, hop, onsite = (pltpu.with_memory_space_constraint(v, pltpu.HBM) for v in operands)
    hbm, vmem = pl.BlockSpec(memory_space=pltpu.HBM), pl.BlockSpec(memory_space=pltpu.VMEM)
    plane = (2, ORB, WIDTH, 8, LANES)
    dma = pltpu.SemaphoreType.DMA
    stats, matrices, lines = pl.pallas_call(
        functools.partial(apply_and_reduce, nx, ny, 1.0 / (ORB * ROWS * LANES * nx * ny)),
        out_shape=tuple(jax.ShapeDtypeStruct(v, f32) for v in ((8, LANES), (2, 2 * WIDTH, LANES)))
        + (jax.ShapeDtypeStruct((ORB, ROWS, 3 * PART, LANES), jnp.bfloat16),),
        in_specs=[hbm] * 6,
        out_specs=(vmem, vmem, vmem),
        scratch_shapes=[
            pltpu.VMEM((ORB, FIELDS, ROWS + 16, LANES), f32),
            pltpu.VMEM((3, ROWS, LANES), i32),
            pltpu.VMEM((ROWS, LANES), i32),
            pltpu.VMEM(hop.shape, f32),
            pltpu.VMEM(onsite.shape, f32),
            pltpu.VMEM((30, 8, LANES), f32),
            pltpu.VMEM((9, ROWS + 8, LANES), f32),
            pltpu.VMEM((9, ROWS, LANES), f32),
            pltpu.VMEM((9, ROWS, LANES), f32),
            pltpu.VMEM((ORB, ROWS, LANES), f32),
            pltpu.VMEM(plane, f32),
            pltpu.VMEM(plane, f32),
            pltpu.VMEM(plane, f32),
            pltpu.VMEM((8, LANES), i32),
            pltpu.VMEM((8, LANES), i32),
            pltpu.VMEM((8, LANES), i32),
            pltpu.VMEM((group_size(STAGES[0]), 2, LANES), f32),
            pltpu.VMEM((group_size(STAGES[1]), 2, LANES), f32),
            pltpu.VMEM((group_size(STAGES[0]), 2, LANES), f32),
            pltpu.VMEM((group_size(STAGES[1]), 2, LANES), f32),
            pltpu.VMEM((6, 32, 8, LANES), f32),
            pltpu.VMEM((FIELDS, 8, LANES), f32),
            pltpu.VMEM((8, LANES), f32),
            dma((6,)),
            dma((6,)),
            dma((6,)),
            dma((4,)),
            dma((4,)),
            pltpu.SemaphoreType.REGULAR((2,)),
        ],
        compiler_params=pltpu.CompilerParams(
            collective_id=0, has_side_effects=True, vmem_limit_bytes=24 << 20
        ),
    )(prev, block, seeds, levels, hop, onsite)
    out, alpha, beta = pl.pallas_call(
        finish,
        out_shape=(
            jax.ShapeDtypeStruct((ORB, WIDTH * ROWS, LANES), f32),
            jax.ShapeDtypeStruct((WIDTH, WIDTH), f32),
            jax.ShapeDtypeStruct((WIDTH, WIDTH), f32),
        ),
        in_specs=[vmem, vmem, vmem],
        out_specs=(hbm, hbm, hbm),
        scratch_shapes=[
            pltpu.VMEM((ORB, WIDTH * ROWS, LANES), f32),
            pltpu.VMEM((WIDTH, 8, LANES), f32),
            pltpu.VMEM((WIDTH, WIDTH), f32),
            pltpu.VMEM((WIDTH, WIDTH), f32),
            dma((ORB + 2,)),
        ],
        compiler_params=pltpu.CompilerParams(vmem_limit_bytes=24 << 20),
    )(lines, stats, matrices)
    return out.reshape(shape), alpha, beta


def solution(mesh):
    fields = P(None, None, "gx", "gy", None)
    return jax.shard_map(
        functools.partial(per_device, mesh.shape["gx"], mesh.shape["gy"]),
        mesh=mesh,
        in_specs=(fields, fields, P(None, "gx", "gy", None), P("gx", "gy", None), P(), P()),
        out_specs=(fields, P(), P()),
        check_vma=False,
    )
```

```python
import functools

import jax
import jax.numpy as jnp
from jax import lax
from jax.experimental import pallas as pl
from jax.experimental.pallas import tpu as pltpu
from jax.sharding import PartitionSpec as P

HIGH = lax.Precision.HIGHEST
MESH = pl.DeviceIdType.MESH
ORB, WIDTH, SIDE, LANES, KINDS = 3, 8, 8, 128, 16
ROWS = SIDE * SIDE
PART = 32
FIELDS = 3 * WIDTH

DIGITS = {"x": 4, "zh": 4, "y": 8, "zl": 2, "core": 2}
STAGES = (("core", "y"), ("x", "zh", "zl"))


def position():
    gx, gy = lax.axis_index("gx"), lax.axis_index("gy")
    return {"x": gx // 4, "zh": gx % 4, "y": gy // 4, "zl": (gy // 2) % 2, "core": gy % 2}


def device(pos):
    return (pos["x"] * 4 + pos["zh"], pos["y"] * 4 + pos["zl"] * 2 + pos["core"])


def group_size(dims):
    size = 1
    for dim in dims:
        size *= DIGITS[dim]
    return size


def member(pos, dims):
    index = 0
    for dim in dims:
        index = index * DIGITS[dim] + pos[dim]
    return index


def offsets(dims):
    found = []
    for k in range(1, group_size(dims)):
        off, rest = {}, k
        for dim in reversed(dims):
            off[dim] = rest % DIGITS[dim]
            rest //= DIGITS[dim]
        hops = 0
        if "y" in off:
            hops += min(off["y"], 8 - off["y"])
        if "x" in off:
            hops += min(off["x"], 4 - off["x"])
        if "zh" in off:
            z = (off["zh"] * 2 + off.get("zl", 0)) % 8
            hops += min(z, 8 - z)
        found.append((-hops, k, off))
    return [off for _, _, off in sorted(found, key=lambda t: t[:2])]


def moved(pos, dim, steps):
    new = dict(pos)
    if dim == "z":
        z = (pos["zh"] * 2 + pos["zl"] + steps) % 8
        new["zh"], new["zl"] = z // 2, z % 2
    else:
        new[dim] = (pos[dim] + steps) % DIGITS[dim]
    return device(new)


def peer(pos, off):
    return {d: (pos[d] + off[d]) % DIGITS[d] if off.get(d) else pos[d] for d in pos}


def iota(axis):
    return lax.broadcasted_iota(jnp.int32, (8, LANES), axis)


def fold_rows(parts):
    row = iota(0)
    for bit in (1, 2, 4):
        low = (row & bit) == 0
        parts = [
            jnp.where(low, a, b) + pltpu.roll(jnp.where(low, b, a), bit, axis=0)
            for a, b in zip(parts[0::2], parts[1::2])
        ]
    return parts[0]


def packed(sums):
    total = sums
    for q in (1, 2, 3):
        total = total + pltpu.roll(pltpu.roll(sums, 8 - 2 * q, axis=0), 32 * q, axis=1)
    return total[0:2, :]


def unpacked(value, spare):
    spare[0:2, :] = value
    for q in (1, 2, 3):
        spare[2 * q : 2 * q + 2, :] = pltpu.roll(value, LANES - 32 * q, axis=1)
    return spare[...]


def products(fields, first, others, planes, acc):
    for x in planes:
        rows = pl.ds(8 * x + 8, 8) if isinstance(x, int) else pl.ds(pl.multiple_of(8 * x + 8, 8), 8)
        for orb in range(ORB):
            left = [fields[orb, first + r, rows, :] for r in range(4)]
            right = [fields[orb, others + s, rows, :] for s in range(8)]
            acc = [acc[r * 8 + s] + left[r] * right[s] for r in range(4) for s in range(8)]
    return acc


def inner_rows(fields, first, others, lane, sums):
    zero = jnp.zeros((8, LANES), jnp.float32)
    acc = lax.fori_loop(0, SIDE, lambda x, acc: tuple(products(fields, first, others, (x,), acc)), (zero,) * 32)
    for r in range(4):
        column = jnp.sum(fold_rows(list(acc[r * 8 : r * 8 + 8])), axis=1, keepdims=True)
        sums = jnp.where(iota(1) == lane + r, column, sums)
    return sums


def terms(value):
    found = []
    for _ in range(3):
        term = value.astype(jnp.bfloat16)
        found.append(term)
        value = value - term.astype(jnp.float32)
    return found


def picked(table, index):
    return jnp.take_along_axis(table, index, axis=1, mode="promise_in_bounds")


def apply_and_reduce(
    nx, ny, scale, prev, block, seeds, levels, hop, onsite, stats, matrices, lines,
    fields, seed_v, level_v, hop_v, onsite_v, table, coef_x, coef_y, coef_z, energy,
    edge_y, halo_x, halo_y, seed_edge, seed_x, seed_y, slots_one, slots_two, early_one, early_two, partial, folded, spare,
    load_sem, halo_send, halo_recv, sum_send, sum_recv, known,
):
    gx, gy = lax.axis_index("gx"), lax.axis_index("gy")
    right, left = ((gx + 1) % nx, gy), ((gx + nx - 1) % nx, gy)
    above, below = (gx, (gy + 1) % ny), (gx, (gy + ny - 1) % ny)
    pos = position()
    plans = [offsets(dims) for dims in STAGES]

    barrier = pltpu.get_barrier_semaphore()
    rings = [moved(pos, dim, k) for dim in ("z", "y") for k in (1, -1, 2, -2)]
    across = [moved(pos, "x", k) for k in (1, 2, 3)] + [moved(pos, "core", 1)]
    partners = [right, left, above, below] + rings + across

    def greet(sem, devices):
        for other in devices:
            pl.semaphore_signal(sem, inc=1, device_id=other, device_id_type=MESH)

    greet(barrier, partners)

    inside = pl.ds(8, ROWS)
    loads = [
        pltpu.make_async_copy(seeds, seed_v, load_sem.at[0]),
        pltpu.make_async_copy(block, fields.at[:, pl.ds(WIDTH, WIDTH), inside, :], load_sem.at[1]),
        pltpu.make_async_copy(hop, hop_v, load_sem.at[2]),
        pltpu.make_async_copy(onsite, onsite_v, load_sem.at[3]),
        pltpu.make_async_copy(levels, level_v, load_sem.at[4]),
        pltpu.make_async_copy(prev, fields.at[:, pl.ds(0, WIDTH), inside, :], load_sem.at[5]),
    ]
    for load in loads:
        load.start()

    pl.semaphore_wait(barrier, len(partners))
    greet(known.at[0], rings)

    def send(i, src, dst, to):
        return pltpu.make_async_remote_copy(
            src_ref=src, dst_ref=dst, send_sem=halo_send.at[i], recv_sem=halo_recv.at[i],
            device_id=to, device_id_type=MESH,
        )

    last, lead = pl.ds(ROWS - 8, 8), pl.ds(0, 8)
    sends = [
        send(0, seeds.at[0, last, :], seed_x, right),
        send(1, block.at[:, :, last, :], halo_x.at[0], right),
        send(2, block.at[:, :, lead, :], halo_x.at[1], left),
    ]
    for copy in sends:
        copy.start()
    loads[0].wait()
    seed_edge[...] = seed_v[1, pl.ds(7, 8, stride=8), :]
    loads[1].wait()

    def pack(n, _):
        for orb in range(ORB):
            edge_y[0, orb, n] = fields[orb, WIDTH + n, pl.ds(15, 8, stride=8), :]
            edge_y[1, orb, n] = fields[orb, WIDTH + n, pl.ds(8, 8, stride=8), :]
        return 0

    lax.fori_loop(0, WIDTH, pack, 0)
    more = [
        send(3, seed_edge, seed_y, above),
        send(4, edge_y.at[0], halo_y.at[0], above),
        send(5, edge_y.at[1], halo_y.at[1], below),
    ]
    for copy in more:
        copy.start()
    sends += more
    pl.semaphore_wait(known.at[0], len(rings))
    greet(known.at[1], across)

    for load in loads[2:5]:
        load.wait()
    zero = jnp.zeros((8, LANES), jnp.float32)

    for a in range(ORB):
        table[27 + a, :, 0:KINDS] = jnp.broadcast_to(onsite_v[a : a + 1, :], (8, KINDS))
        for d in range(3):
            for b in range(ORB):
                table[d * 9 + a * 3 + b, :, 0:KINDS] = jnp.broadcast_to(hop_v[d, a, b : b + 1, :], (8, KINDS))

    for n in range(WIDTH):
        for orb in range(ORB):
            fields[orb, WIDTH + n, 0:8, :] = zero
            fields[orb, WIDTH + n, ROWS + 8 : ROWS + 16, :] = zero
    for ab in range(9):
        coef_x[ab, 0:8, :] = zero
    inner_row = iota(0) < 7

    def look_up(x, _):
        rows = pl.ds(pl.multiple_of(8 * x, 8), 8)
        later = pl.ds(pl.multiple_of(8 * x + 8, 8), 8)
        at_x, at_y, at_z = (seed_v[d, rows, :] for d in range(3))
        level = level_v[rows, :]
        for a in range(ORB):
            energy[a, rows, :] = picked(table[27 + a], level)
            for b in range(ORB):
                ab = a * 3 + b
                coef_x[ab, later, :] = picked(table[ab], at_x)
                coef_y[ab, rows, :] = jnp.where(inner_row, picked(table[9 + ab], at_y), 0.0)
                coef_z[ab, rows, :] = picked(table[18 + ab], at_z)
        return 0

    lax.fori_loop(0, SIDE, look_up, 0)

    def own(x, _):
        before = pl.ds(pl.multiple_of(8 * x, 8), 8)
        here = pl.ds(pl.multiple_of(8 * x + 8, 8), 8)
        after = pl.ds(pl.multiple_of(8 * x + 16, 8), 8)
        cx = [coef_x[ab, here, :] for ab in range(9)]
        cm = [coef_x[ab, before, :] for ab in range(9)]
        cy = [coef_y[ab, before, :] for ab in range(9)]
        cz = [coef_z[ab, before, :] for ab in range(9)]
        ce = [energy[a, before, :] for a in range(ORB)]
        for n in range(WIDTH):
            v = [fields[b, WIDTH + n, here, :] for b in range(ORB)]
            vp = [fields[b, WIDTH + n, after, :] for b in range(ORB)]
            vm = [fields[b, WIDTH + n, before, :] for b in range(ORB)]
            vz = [pltpu.roll(u, LANES - 1, axis=1) for u in v]
            vy = [pltpu.roll(u, 7, axis=0) for u in v]
            for a in range(ORB):
                carried_z = cz[a] * v[0] + cz[3 + a] * v[1] + cz[6 + a] * v[2]
                carried_y = cy[a] * v[0] + cy[3 + a] * v[1] + cy[6 + a] * v[2]
                out = ce[a] * v[a] + pltpu.roll(carried_z, 1, axis=1) + pltpu.roll(carried_y, 1, axis=0)
                for b in range(ORB):
                    out = out + cx[a * 3 + b] * vp[b] + cm[b * 3 + a] * vm[b]
                    out = out + cz[a * 3 + b] * vz[b] + cy[a * 3 + b] * vy[b]
                fields[a, 2 * WIDTH + n, here, :] = out
        return 0

    lax.fori_loop(0, SIDE, own, 0)

    def share(stage, slots, sem, value):
        me = member(pos, STAGES[stage])
        slots[me] = value
        for off in plans[stage]:
            pltpu.make_async_remote_copy(
                src_ref=slots.at[me], dst_ref=slots.at[me], send_sem=sum_send.at[sem], recv_sem=sum_recv.at[sem],
                device_id=device(peer(pos, off)), device_id_type=MESH,
            ).start()

    def bulk_wait(stage, slots, sems):
        bulk = slots.at[pl.ds(0, group_size(STAGES[stage]) - 1)]
        pltpu.make_async_copy(bulk, bulk, sems).wait()

    def gathered(stage, slots, sem):
        bulk_wait(stage, slots, sum_recv.at[sem])
        value = slots[0]
        for k in range(1, group_size(STAGES[stage])):
            value = value + slots[k]
        return value

    loads[5].wait()

    def basis_rows(i, sums):
        sums = inner_rows(fields, 4 * i, 0, 4 * i, sums)
        return inner_rows(fields, 4 * i, WIDTH, 16 + 4 * i, sums)

    sums = lax.fori_loop(0, 4, basis_rows, zero)
    early = packed(sums)

    for i in (3, 4, 5):
        sends[i].wait_recv()
    cb = [picked(table[9 + ab], seed_y[...]) for ab in range(9)]
    cf = [picked(table[9 + ab], seed_edge[...]) for ab in range(9)]

    def edges_y(n, _):
        for a in range(ORB):
            field = fields.at[a, 2 * WIDTH + n]
            low, high = field[pl.ds(8, 8, stride=8), :], field[pl.ds(15, 8, stride=8), :]
            for b in range(ORB):
                low = low + cb[b * 3 + a] * halo_y[0, b, n]
                high = high + cf[a * 3 + b] * halo_y[1, b, n]
            field[pl.ds(8, 8, stride=8), :] = low
            field[pl.ds(15, 8, stride=8), :] = high
        return 0

    lax.fori_loop(0, WIDTH, edges_y, 0)

    def inner_planes(i, _):
        acc = lax.fori_loop(
            1, SIDE - 1, lambda x, acc: tuple(products(fields, 4 * i, 2 * WIDTH, (x,), acc)), (zero,) * 32
        )
        for k in range(32):
            partial[i, k] = acc[k]
        return 0

    lax.fori_loop(0, 6, inner_planes, 0)
    pl.semaphore_wait(known.at[1], len(across))
    share(0, early_one, 2, early)

    for i in (0, 1, 2):
        sends[i].wait_recv()
    cm = [picked(table[ab], seed_x[...]) for ab in range(9)]
    cp = [coef_x[ab, ROWS : ROWS + 8, :] for ab in range(9)]

    def edges_x(n, _):
        for a in range(ORB):
            field = fields.at[a, 2 * WIDTH + n]
            low, high = field[8:16, :], field[ROWS : ROWS + 8, :]
            for b in range(ORB):
                low = low + cm[b * 3 + a] * halo_x[0, b, n]
                high = high + cp[a * 3 + b] * halo_x[1, b, n]
            field[8:16, :] = low
            field[ROWS : ROWS + 8, :] = high
        return 0

    for n in range(WIDTH):
        edges_x(n, 0)

    def outer_planes(i, _):
        acc = products(fields, 4 * i, 2 * WIDTH, (0, SIDE - 1), [partial[i, k] for k in range(32)])
        for r in range(4):
            folded[4 * i + r] = fold_rows(acc[r * 8 : r * 8 + 8])
        return 0

    for i in range(6):
        outer_planes(i, 0)
    sums = zero
    for k in range(FIELDS):
        sums = jnp.where(iota(1) == k, jnp.sum(folded[k], axis=1, keepdims=True), sums)
    share(0, slots_one, 0, packed(sums))

    flat = fields.reshape(ORB, FIELDS * (ROWS + 16), LANES)
    padding = jnp.zeros((PART - FIELDS, LANES), jnp.float32)

    def line_terms(orb):
        def step(x, _):
            for y in range(8):
                value = flat[orb, pl.ds(8 * x + 8 + y, FIELDS, stride=ROWS + 16), :]
                value = jnp.concatenate([value, padding], axis=0)
                for i, term in enumerate(terms(value)):
                    lines[orb, 8 * x + y, i * PART : (i + 1) * PART, :] = term
            return 0

        lax.fori_loop(0, SIDE, step, 0)

    line_terms(0)
    share(1, early_two, 3, gathered(0, early_one, 2))

    share(1, slots_two, 1, gathered(0, slots_one, 0))
    line_terms(1)
    line_terms(2)

    both = unpacked(gathered(1, early_two, 3), spare) * scale
    row, lane = iota(0), iota(1)
    metric = [jnp.where(lane < 16, both, 0.0), jnp.where(lane < 16, pltpu.roll(both, LANES - 16, axis=1), 0.0)]
    twice = [jnp.where(row + 8 * i == lane, 2.0, 0.0) - metric[i] for i in range(2)]
    metric, twice = (jnp.concatenate(m, axis=0) for m in (metric, twice))
    matrices[0] = twice
    matrices[1] = 2.0 * twice - rows_dot(rows_dot(twice, metric), twice)

    stats[...] = unpacked(gathered(1, slots_two, 1), spare) * scale
    for copy in sends:
        copy.wait_send()
    for sem, slots in enumerate((slots_one, slots_two, early_one, early_two)):
        bulk_wait(sem % 2, slots, sum_send.at[sem])


def wide(matrix):
    return jnp.concatenate([matrix, jnp.zeros((LANES - matrix.shape[0], LANES), jnp.float32)], axis=0)


def rows_dot(left, right):
    return lax.dot_general(
        left, wide(right), (((1,), (1,)), ((), ())), precision=HIGH, preferred_element_type=jnp.float32
    )


def finish(
    lines, stats, matrices, out, alpha, beta,
    result, columns, alpha_v, beta_v, store_sem,
):
    row, lane = iota(0), iota(1)
    first = jnp.where(lane < 16, stats[...], 0.0)
    norms = jnp.where(lane < 8, pltpu.roll(stats[...], LANES - 16, axis=1), 0.0)
    coeffs = rows_dot(first, matrices[0])
    last = jnp.where(lane < 8, pltpu.roll(first, LANES - 8, axis=1), 0.0)
    unit = jnp.where(row == lane, 1.0, 0.0)
    alpha_v[...] = rows_dot(unit, last)[:, 0:WIDTH]
    stores = [pltpu.make_async_copy(alpha_v, alpha, store_sem.at[ORB])]
    stores[0].start()
    gram = norms - rows_dot(rows_dot(first, matrices[1]), first)
    for j in range(WIDTH):
        columns[j] = jnp.broadcast_to(gram[:, j : j + 1], (8, LANES))

    a = [[jnp.broadcast_to(columns[j, i : i + 1, :], (8, LANES)) for j in range(i + 1)] for i in range(WIDTH)]
    inverse = [[None] * WIDTH for _ in range(WIDTH)]
    upper = jnp.zeros((8, LANES), jnp.float32)
    for j in range(WIDTH):
        inverse[j][j] = lax.rsqrt(a[j][j])
        for i in range(j, WIDTH):
            a[i][j] = a[i][j] * inverse[j][j]
            upper = jnp.where((row == j) & (lane == i), a[i][j], upper)
        for i in range(j + 1, WIDTH):
            for k in range(j + 1, i + 1):
                a[i][k] = a[i][k] - a[i][j] * a[k][j]
    for i in range(WIDTH):
        for j in range(i):
            total = a[i][j] * inverse[j][j]
            for k in range(j + 1, i):
                total = total + a[i][k] * inverse[k][j]
            inverse[i][j] = -(total * inverse[i][i])
    beta_v[...] = upper[:, 0:WIDTH]
    stores.append(pltpu.make_async_copy(beta_v, beta, store_sem.at[ORB + 1]))
    stores[1].start()
    weights = jnp.zeros((8, LANES), jnp.float32)
    for m in range(WIDTH):
        column = jnp.zeros((8, LANES), jnp.float32)
        for n in range(m, WIDTH):
            column = jnp.where(row == n, inverse[n][m], column)
        weights = weights - column * jnp.broadcast_to(coeffs[m : m + 1, :], (8, LANES))
        weights = jnp.where(lane == 2 * WIDTH + m, column, weights)
    high, middle, low = (term.astype(jnp.float32) for term in terms(weights))
    shifted = [[pltpu.roll(t, PART * i, axis=1) if i else t for i in range(c)] for t, c in ((high, 3), (middle, 2), (low, 1))]
    matrix = jnp.concatenate([sum(group[1:], group[0]) for group in shifted], axis=0).astype(jnp.bfloat16)
    matrix = matrix[:, : 3 * PART]

    for orb in range(ORB):

        for x in range(SIDE):
            for y in range(0, 8, 2):
                pair = jnp.concatenate([lines[orb, 8 * x + y + i] for i in range(2)], axis=1)
                got = jnp.dot(matrix, pair, preferred_element_type=jnp.float32)
                got = got[0:8] + got[8:16] + got[16:24]
                for i in range(2):
                    result[orb, pl.ds(8 * x + y + i, 8, stride=ROWS), :] = got[:, i * LANES : (i + 1) * LANES]
        stores.append(pltpu.make_async_copy(result.at[orb], out.at[orb], store_sem.at[orb]))
        stores[-1].start()
    for store in stores:
        store.wait()


def per_device(nx, ny, prev, block, seeds, levels, hop, onsite):
    f32, i32 = jnp.float32, jnp.int32
    shape = block.shape
    prev, block = (v.reshape(ORB, WIDTH, ROWS, LANES) for v in (prev, block))
    hop, onsite = hop.transpose(0, 2, 3, 1), onsite.T
    seeds, levels = seeds.reshape(3, ROWS, LANES), levels.reshape(ROWS, LANES)
    operands = (prev, block, seeds, levels, hop, onsite)
    prev, block, seeds, levels, hop, onsite = (pltpu.with_memory_space_constraint(v, pltpu.HBM) for v in operands)
    hbm, vmem = pl.BlockSpec(memory_space=pltpu.HBM), pl.BlockSpec(memory_space=pltpu.VMEM)
    plane = (2, ORB, WIDTH, 8, LANES)
    dma = pltpu.SemaphoreType.DMA
    stats, matrices, lines = pl.pallas_call(
        functools.partial(apply_and_reduce, nx, ny, 1.0 / (ORB * ROWS * LANES * nx * ny)),
        out_shape=tuple(jax.ShapeDtypeStruct(v, f32) for v in ((8, LANES), (2, 2 * WIDTH, LANES)))
        + (jax.ShapeDtypeStruct((ORB, ROWS, 3 * PART, LANES), jnp.bfloat16),),
        in_specs=[hbm] * 6,
        out_specs=(vmem, vmem, vmem),
        scratch_shapes=[
            pltpu.VMEM((ORB, FIELDS, ROWS + 16, LANES), f32),
            pltpu.VMEM((3, ROWS, LANES), i32),
            pltpu.VMEM((ROWS, LANES), i32),
            pltpu.VMEM(hop.shape, f32),
            pltpu.VMEM(onsite.shape, f32),
            pltpu.VMEM((30, 8, LANES), f32),
            pltpu.VMEM((9, ROWS + 8, LANES), f32),
            pltpu.VMEM((9, ROWS, LANES), f32),
            pltpu.VMEM((9, ROWS, LANES), f32),
            pltpu.VMEM((ORB, ROWS, LANES), f32),
            pltpu.VMEM(plane, f32),
            pltpu.VMEM(plane, f32),
            pltpu.VMEM(plane, f32),
            pltpu.VMEM((8, LANES), i32),
            pltpu.VMEM((8, LANES), i32),
            pltpu.VMEM((8, LANES), i32),
            pltpu.VMEM((group_size(STAGES[0]), 2, LANES), f32),
            pltpu.VMEM((group_size(STAGES[1]), 2, LANES), f32),
            pltpu.VMEM((group_size(STAGES[0]), 2, LANES), f32),
            pltpu.VMEM((group_size(STAGES[1]), 2, LANES), f32),
            pltpu.VMEM((6, 32, 8, LANES), f32),
            pltpu.VMEM((FIELDS, 8, LANES), f32),
            pltpu.VMEM((8, LANES), f32),
            dma((6,)),
            dma((6,)),
            dma((6,)),
            dma((4,)),
            dma((4,)),
            pltpu.SemaphoreType.REGULAR((2,)),
        ],
        compiler_params=pltpu.CompilerParams(
            collective_id=0, has_side_effects=True, vmem_limit_bytes=24 << 20
        ),
    )(prev, block, seeds, levels, hop, onsite)
    out, alpha, beta = pl.pallas_call(
        finish,
        out_shape=(
            jax.ShapeDtypeStruct((ORB, WIDTH * ROWS, LANES), f32),
            jax.ShapeDtypeStruct((WIDTH, WIDTH), f32),
            jax.ShapeDtypeStruct((WIDTH, WIDTH), f32),
        ),
        in_specs=[vmem, vmem, vmem],
        out_specs=(hbm, hbm, hbm),
        scratch_shapes=[
            pltpu.VMEM((ORB, WIDTH * ROWS, LANES), f32),
            pltpu.VMEM((WIDTH, 8, LANES), f32),
            pltpu.VMEM((WIDTH, WIDTH), f32),
            pltpu.VMEM((WIDTH, WIDTH), f32),
            dma((ORB + 2,)),
        ],
        compiler_params=pltpu.CompilerParams(vmem_limit_bytes=24 << 20),
    )(lines, stats, matrices)
    return out.reshape(shape), alpha, beta


def solution(mesh):
    fields = P(None, None, "gx", "gy", None)
    return jax.shard_map(
        functools.partial(per_device, mesh.shape["gx"], mesh.shape["gy"]),
        mesh=mesh,
        in_specs=(fields, fields, P(None, "gx", "gy", None), P("gx", "gy", None), P(), P()),
        out_specs=(fields, P(), P()),
        check_vma=False,
    )
```
